32 devices in a mesh: blk: 8 (over z, x), grp: 4 (over y, core).
Axes of the slice: x: 2, y: 2, z: 4, core: 2. Of those that a mesh axis runs over, the one named last changes fastest.
Arguments:
- image: bfloat16 [4, 8, 32768], P('grp', 'blk'), may hold values from -6 to 6
- context: bfloat16 [4, 1024, 128], P('grp'), may hold values from -6 to 6
- tissue: int32 [4, 8], P('grp'), may hold values from 0 to 15, as said below
- owner: int32 [4, 8], P('grp'), may hold values from 0 to 7, as said below
- neighbours: int32 [4, 8, 6], P('grp', 'blk'), may hold values from -1 to 7, as said below
- w_in: bfloat16 [7, 64, 1], replicated, may hold values from -2 to 2
- b_in: float32 [64], replicated, may hold values from -1.75 to 1.75
- w_down: bfloat16 [7, 128, 64], replicated, may hold values from -0.25 to 0.25
- b_down: float32 [128], replicated, may hold values from -1.75 to 1.75
- w_ctx: bfloat16 [7, 128, 128], replicated, may hold values from -0.1875 to 0.1875
- w_mid: bfloat16 [7, 128, 128], replicated, may hold values from -0.1875 to 0.1875
- b_mid: float32 [128], replicated, may hold values from -1.75 to 1.75
- w_skip: bfloat16 [128, 64], replicated, may hold values from -0.4375 to 0.4375
- w_lift: bfloat16 [128, 128], replicated, may hold values from -0.4375 to 0.4375
- b_up: float32 [128], replicated, may hold values from -1.75 to 1.75
- w_out: bfloat16 [3, 128], replicated, may hold values from -1 to 1
- b_out: float32 [3], replicated, may hold values from -3 to 3
Outputs:
- affinity: float32 [4, 8, 3, 32768], P('grp', 'blk')
The draws below stay inside these ranges and needn't reach their ends.
Inputs may be any that keep to these rules, and one draw needn't show every extreme that they name: tissue[g] is the 8 consecutive positions of two adjacent x layers of section g. owner[g, j] = (j + r_g) mod 8 for a shift r_g of section g. neighbours[g, d, k] is the owner of the kept block next to device d's block in direction k within section g, -1 where that position is outside the section or not kept.
All inputs are finite; a program needn't handle non-finite values.
Results may differ from the reference program's by a relative error of at most 0.004.
Values may be sent and summed in bfloat16 or wider, within the bound.
No kernel may reach another device: no remote copies, remote signals or barrier semaphores. Data moves between devices by JAX's collectives and lax.ppermute only.
A program may use at most 64 MiB of HBM per device.

```python
import jax
import jax.numpy as jnp
from jax import lax

E = 32
C0 = 64
C1 = 128
CC = 128
K = 4
ZR = 1
CTX_CELLS = 1024
N_BLK = 8
N_GRP = 4


def geometry(key):
    depth = N_BLK // 8
    base = jax.random.fold_in(key, 7)
    layer = jax.random.randint(jax.random.fold_in(base, 1), (N_GRP,), 0, 3).astype(jnp.int32)
    sections = jnp.arange(N_GRP, dtype=jnp.int32)
    layer = jnp.where(sections == 0, 2, jnp.where(sections == 1, 0, layer)).astype(jnp.int32)
    rotate = jax.random.randint(jax.random.fold_in(base, 2), (N_GRP,), 0, N_BLK).astype(jnp.int32)
    slots = jnp.arange(N_BLK, dtype=jnp.int32)
    tissue = (layer[:, None] * (4 * depth) + slots[None, :]).astype(jnp.int32)
    owner = ((slots[None, :] + rotate[:, None]) % N_BLK).astype(jnp.int32)
    which = ((slots[None, :] - rotate[:, None]) % N_BLK).astype(jnp.int32)
    pos = jnp.take_along_axis(tissue, which, axis=1)
    bx = pos // (4 * depth)
    by = pos // depth % 4
    bz = pos % depth
    dx = jnp.array([-1, 1, 0, 0, 0, 0], jnp.int32)
    dy = jnp.array([0, 0, -1, 1, 0, 0], jnp.int32)
    dz = jnp.array([0, 0, 0, 0, -1, 1], jnp.int32)
    nx = bx[:, :, None] + dx
    ny = by[:, :, None] + dy
    nz = bz[:, :, None] + dz
    inside = (nx >= 0) & (nx < 4) & (ny >= 0) & (ny < 4) & (nz >= 0) & (nz < depth)
    target = nz + depth * (ny + 4 * nx)
    match = tissue[:, None, None, :] == target[:, :, :, None]
    found = jnp.any(match, axis=-1) & inside
    device = jnp.sum(jnp.where(match, owner[:, None, None, :], 0), axis=-1)
    neighbours = jnp.where(found, device, -1).astype(jnp.int32)
    return (tissue, owner, neighbours)


def draw_tissue(key, part):
    return geometry(key)[0]


def draw_owner(key, part):
    return geometry(key)[1]


def draw_neighbours(key, part):
    return geometry(key)[2]


def block_levels(key, extent, cuts, least, top_value):
    level = 1.0
    for position, parts in cuts:
        heights = jax.random.uniform(jax.random.fold_in(jax.random.fold_in(key, 6), position), (parts,), jnp.float32, least / len(cuts), top_value / len(cuts))
        level = level * jnp.repeat(jnp.exp(heights), extent[position] // parts).reshape((-1,) + (1,) * (len(extent) - 1 - position))
    return level


def bell_draw(stream_key, shape, width, reach, cuts=(), kind=jnp.bfloat16):
    gain = block_levels(stream_key, shape, cuts, -0.22, 0.18) if cuts else 1.0
    values = jax.random.normal(stream_key, shape, jnp.float32) * width * gain
    return jnp.minimum(jnp.maximum(values, -reach), reach).astype(kind)


def setup_inputs(seed: int = 0) -> dict:
    keys = jax.random.split(jax.random.key(seed), 18)
    image = bell_draw(keys[0], (N_GRP, N_BLK, E ** 3), 1.0, 6.0, ((0, 4), (1, 8)))
    context = bell_draw(keys[1], (N_GRP, CTX_CELLS, CC), 1.0, 6.0, ((0, 4),))
    tissue = draw_tissue(jax.random.fold_in(keys[17], 71), 0)
    owner = draw_owner(jax.random.fold_in(keys[17], 71), 0)
    neighbours = draw_neighbours(jax.random.fold_in(keys[17], 71), 0)
    w_in = bell_draw(keys[5], (7, C0, 1), 7 ** -0.5, 2.0)
    b_in = bell_draw(keys[6], (C0,), 0.3, 1.75, (), jnp.float32)
    w_down = bell_draw(keys[7], (7, C1, C0), (7 * C0) ** -0.5, 0.25)
    b_down = bell_draw(keys[8], (C1,), 0.3, 1.75, (), jnp.float32)
    w_ctx = bell_draw(keys[9], (7, CC, C1), (7 * CC) ** -0.5, 0.1875)
    w_mid = bell_draw(keys[10], (7, C1, C1), (7 * C1) ** -0.5, 0.1875)
    b_mid = bell_draw(keys[11], (C1,), 0.3, 1.75, (), jnp.float32)
    w_skip = bell_draw(keys[12], (C1, C0), (C0 + C1) ** -0.5, 0.4375)
    w_lift = bell_draw(keys[13], (C1, C1), (C0 + C1) ** -0.5, 0.4375)
    b_up = bell_draw(keys[14], (C1,), 0.3, 1.75, (), jnp.float32)
    w_out = bell_draw(keys[15], (3, C1), (C1 // 4) ** -0.5, 1.0)
    b_out = bell_draw(keys[16], (3,), 0.5, 3.0, (), jnp.float32)
    return dict(image=image, context=context, tissue=tissue, owner=owner, neighbours=neighbours, w_in=w_in, b_in=b_in, w_down=w_down, b_down=b_down, w_ctx=w_ctx, w_mid=w_mid, b_mid=b_mid, w_skip=w_skip, w_lift=w_lift, b_up=b_up, w_out=w_out, b_out=b_out)


def faces_of(x):
    return jnp.stack([x[:, 0], x[:, -1], x[:, :, 0], x[:, :, -1], x[:, :, :, 0], x[:, :, :, -1]])


def conv_taps(x, halos, weight):
    chans = x.shape[0]
    views = [x,
             jnp.concatenate([halos[0][:, None], x[:, :-1]], 1),
             jnp.concatenate([x[:, 1:], halos[1][:, None]], 1),
             jnp.concatenate([halos[2][:, :, None], x[:, :, :-1]], 2),
             jnp.concatenate([x[:, :, 1:], halos[3][:, :, None]], 2),
             jnp.concatenate([halos[4][:, :, :, None], x[:, :, :, :-1]], 3),
             jnp.concatenate([x[:, :, :, 1:], halos[5][:, :, :, None]], 3)]
    total = jnp.dot(weight[0], views[0].reshape(chans, -1), preferred_element_type=jnp.float32)
    for tap in range(1, 7):
        total = total + jnp.dot(weight[tap], views[tap].reshape(chans, -1), preferred_element_type=jnp.float32)
    return total


def upsample(v, factor):
    chans, side = v.shape[0], v.shape[1]
    big = jnp.broadcast_to(v[:, :, None, :, None, :, None], (chans, side, factor, side, factor, side, factor))
    return big.reshape(chans, side * factor, side * factor, side * factor)


def pooled(a0, edge):
    half = edge // 2
    return a0.reshape(a0.shape[0], half, 2, half, 2, half, 2).max(axis=(2, 4, 6))


def context_term(near, bx, by, bz, w_ctx, coarse, depth_blocks):
    side = 4 * coarse
    chans = near.shape[-1]
    regions = near.reshape(3, side, side, depth_blocks * coarse, chans)
    middle = jnp.pad(regions[1], ((coarse, coarse), (coarse, coarse), (0, 0), (0, 0)))
    zoff = (bz * coarse).astype(jnp.int32)
    xoff = (bx * coarse).astype(jnp.int32)
    yoff = (by * coarse).astype(jnp.int32)
    zero = jnp.zeros((), jnp.int32)
    size = (coarse, coarse, coarse, chans)
    shift = jnp.int32(coarse)
    taps = [lax.dynamic_slice(middle, (xoff + shift, yoff + shift, zoff, zero), size),
            lax.dynamic_slice(middle, (xoff, yoff + shift, zoff, zero), size),
            lax.dynamic_slice(middle, (xoff + 2 * shift, yoff + shift, zoff, zero), size),
            lax.dynamic_slice(middle, (xoff + shift, yoff, zoff, zero), size),
            lax.dynamic_slice(middle, (xoff + shift, yoff + 2 * shift, zoff, zero), size),
            lax.dynamic_slice(regions[0], (xoff, yoff, zoff, zero), size),
            lax.dynamic_slice(regions[2], (xoff, yoff, zoff, zero), size)]
    total = jnp.dot(taps[0].reshape(-1, chans), w_ctx[0], preferred_element_type=jnp.float32)
    for tap in range(1, 7):
        total = total + jnp.dot(taps[tap].reshape(-1, chans), w_ctx[tap], preferred_element_type=jnp.float32)
    return total.T.reshape(-1, coarse, coarse, coarse)


def reference(image, context, tissue, owner, neighbours, w_in, b_in, w_down, b_down, w_ctx, w_mid, b_mid, w_skip, w_lift, b_up, w_out, b_out):
    half = E // 2
    total = N_GRP * N_BLK
    opposite = jnp.bitwise_xor(jnp.arange(6, dtype=jnp.int32), jnp.int32(1))
    volume = image.reshape(N_GRP, N_BLK, 1, E, E, E)
    img_faces = jax.vmap(jax.vmap(faces_of))(volume)

    def halos_for(faces_all, g, d):
        nbr = neighbours[g, d]
        safe = jnp.maximum(nbr, 0)
        picked = faces_all[g][safe, opposite]
        mask = (nbr >= 0).astype(picked.dtype)
        return picked * mask[:, None, None, None]

    def level_zero(g, d):
        pre = conv_taps(volume[g, d], halos_for(img_faces, g, d), w_in) + b_in[:, None]
        return jnp.maximum(pre, 0.0).astype(jnp.bfloat16).reshape(-1, E, E, E)

    def split(i):
        return i // N_BLK, i % N_BLK

    index = jnp.arange(total, dtype=jnp.int32)

    def segment_a(i):
        g, d = split(i)
        return pooled(level_zero(g, d), E)

    p1 = lax.map(segment_a, index).reshape(N_GRP, N_BLK, -1, half, half, half)
    p1_faces = jax.vmap(jax.vmap(faces_of))(p1)

    def segment_b(i):
        g, d = split(i)
        pre = conv_taps(p1[g, d], halos_for(p1_faces, g, d), w_down) + b_down[:, None]
        return jnp.maximum(pre, 0.0).astype(jnp.bfloat16).reshape(-1, half, half, half)

    a1 = lax.map(segment_b, index).reshape(N_GRP, N_BLK, -1, half, half, half)
    a1_faces = jax.vmap(jax.vmap(faces_of))(a1)
    ctx_pad = jnp.pad(context, ((1, 1), (0, 0), (0, 0)))

    def segment_c(i):
        g, d = split(i)
        a0 = level_zero(g, d)
        pos = jnp.sum(jnp.where(owner[g] == d, tissue[g], 0)).astype(jnp.int32)
        bx = pos // (4 * ZR)
        by = (pos // ZR) % 4
        bz = pos % ZR
        near = lax.dynamic_slice_in_dim(ctx_pad, g, 3, 0)
        cterm = context_term(near, bx, by, bz, w_ctx, K, ZR)
        pre = conv_taps(a1[g, d], halos_for(a1_faces, g, d), w_mid) + b_mid[:, None]
        pre = pre + upsample(cterm, 4).reshape(cterm.shape[0], -1)
        a2 = jnp.maximum(pre, 0.0).astype(jnp.bfloat16)
        lifted = jnp.dot(w_lift, a2, preferred_element_type=jnp.float32).reshape(-1, half, half, half)
        mixed = upsample(lifted, 2).reshape(lifted.shape[0], -1)
        mixed = mixed + jnp.dot(w_skip, a0.reshape(a0.shape[0], -1), preferred_element_type=jnp.float32) + b_up[:, None]
        hidden = jnp.maximum(mixed, 0.0).astype(jnp.bfloat16)
        logits = jnp.dot(w_out, hidden, preferred_element_type=jnp.float32) + b_out[:, None]
        return jax.nn.sigmoid(logits)

    result = lax.map(segment_c, index)
    return result.reshape(N_GRP, N_BLK, 3, E * E * E)
```

```python
import jax
import jax.numpy as jnp
from jax import lax
from jax.experimental import pallas as pl
from jax.experimental.pallas import tpu as pltpu
from jax.sharding import PartitionSpec as P

E = 32


def from_behind(shard, axis, by):
    devices = lax.axis_size(axis)
    return lax.ppermute(shard, axis, [(i, (i + by) % devices) for i in range(devices)])


def extended(shard, sides, width):
    for axis, dim in sides:
        devices, length = (lax.axis_size(axis), shard.shape[dim])
        up = [(i, (i + 1) % devices) for i in range(devices - 1)]
        down = [(j, i) for i, j in up]
        last = lax.slice_in_dim(shard, length - width, length, axis=dim)
        initial = lax.slice_in_dim(shard, 0, width, axis=dim)
        before = lax.ppermute(last, axis, up)
        after = lax.ppermute(initial, axis, down)
        shard = jnp.concatenate([before, shard, after], axis=dim)
    return shard


def faces_of(x):
    return jnp.stack([x[:, 0], x[:, -1], x[:, :, 0], x[:, :, -1], x[:, :, :, 0], x[:, :, :, -1]])


def conv_taps(x, halos, weight):
    chans = x.shape[0]
    views = [
        x,
        jnp.concatenate([halos[0][:, None], x[:, :-1]], 1),
        jnp.concatenate([x[:, 1:], halos[1][:, None]], 1),
        jnp.concatenate([halos[2][:, :, None], x[:, :, :-1]], 2),
        jnp.concatenate([x[:, :, 1:], halos[3][:, :, None]], 2),
        jnp.concatenate([halos[4][:, :, :, None], x[:, :, :, :-1]], 3),
        jnp.concatenate([x[:, :, :, 1:], halos[5][:, :, :, None]], 3),
    ]
    total = jnp.dot(weight[0], views[0].reshape(chans, -1), preferred_element_type=jnp.float32)
    for tap in range(1, 7):
        total = total + jnp.dot(
            weight[tap], views[tap].reshape(chans, -1), preferred_element_type=jnp.float32
        )
    return total


def upsample(v, factor):
    chans, side = (v.shape[0], v.shape[1])
    big = jnp.broadcast_to(
        v[:, :, None, :, None, :, None], (chans, side, factor, side, factor, side, factor)
    )
    return big.reshape(chans, side * factor, side * factor, side * factor)


def pooled(a0):
    half = a0.shape[1] // 2
    return a0.reshape(a0.shape[0], half, 2, half, 2, half, 2).max(axis=(2, 4, 6))


def neighbour_faces(x, nbr):
    flat = faces_of(x)
    count = lax.axis_size("blk")
    depth_blocks = count // 8
    offsets = [-(count // 2), count // 2, -depth_blocks, depth_blocks, -1, 1]
    pieces = []
    for direction in range(6):
        pieces.append(from_behind(flat[direction ^ 1], "blk", -offsets[direction]))
    mask = (nbr >= 0).astype(jnp.bfloat16)
    return jnp.stack(pieces) * mask[:, None, None, None]


def context_term(near, bx, by, bz, w_ctx, coarse, depth_blocks):
    side = 4 * coarse
    chans = near.shape[-1]
    regions = near.reshape(3, side, side, depth_blocks * coarse, chans)
    middle = jnp.pad(regions[1], ((coarse, coarse), (coarse, coarse), (0, 0), (0, 0)))
    zoff = bz * coarse
    xoff = bx * coarse
    yoff = by * coarse
    zero = jnp.zeros((), jnp.int32)
    size = (coarse, coarse, coarse, chans)
    shift = jnp.int32(coarse)
    taps = [
        lax.dynamic_slice(middle, (xoff + shift, yoff + shift, zoff, zero), size),
        lax.dynamic_slice(middle, (xoff, yoff + shift, zoff, zero), size),
        lax.dynamic_slice(middle, (xoff + 2 * shift, yoff + shift, zoff, zero), size),
        lax.dynamic_slice(middle, (xoff + shift, yoff, zoff, zero), size),
        lax.dynamic_slice(middle, (xoff + shift, yoff + 2 * shift, zoff, zero), size),
        lax.dynamic_slice(regions[0], (xoff, yoff, zoff, zero), size),
        lax.dynamic_slice(regions[2], (xoff, yoff, zoff, zero), size),
    ]
    total = jnp.dot(taps[0].reshape(-1, chans), w_ctx[0], preferred_element_type=jnp.float32)
    for tap in range(1, 7):
        total = total + jnp.dot(
            taps[tap].reshape(-1, chans), w_ctx[tap], preferred_element_type=jnp.float32
        )
    return total.T.reshape(-1, coarse, coarse, coarse)


def layered_shards(
    image,
    context,
    tissue,
    owner,
    neighbours,
    w_in,
    b_in,
    w_down,
    b_down,
    w_ctx,
    w_mid,
    b_mid,
    w_skip,
    w_lift,
    b_up,
    w_out,
    b_out,
):
    half = E // 2
    coarse = E // 8
    depth_blocks = tissue.shape[1] // 8
    nbr = neighbours[0, 0]
    volume = image.reshape(1, E, E, E)
    pre = conv_taps(volume, neighbour_faces(volume, nbr), w_in) + b_in[:, None]
    a0 = jnp.maximum(pre, 0.0).astype(jnp.bfloat16).reshape(-1, E, E, E)
    p1 = pooled(a0)
    pre = conv_taps(p1, neighbour_faces(p1, nbr), w_down) + b_down[:, None]
    a1 = jnp.maximum(pre, 0.0).astype(jnp.bfloat16).reshape(-1, half, half, half)
    me = lax.axis_index("blk")
    pos = jnp.sum(jnp.where(owner[0] == me, tissue[0], 0))
    bx = pos // (4 * depth_blocks)
    by = pos // depth_blocks % 4
    bz = pos % depth_blocks
    near = extended(context, (("grp", 0),), 1)
    cterm = context_term(near, bx, by, bz, w_ctx, coarse, depth_blocks)
    pre = conv_taps(a1, neighbour_faces(a1, nbr), w_mid) + b_mid[:, None]
    pre = pre + upsample(cterm, 4).reshape(cterm.shape[0], -1)
    a2 = jnp.maximum(pre, 0.0).astype(jnp.bfloat16)
    lifted = jnp.dot(w_lift, a2, preferred_element_type=jnp.float32).reshape(-1, half, half, half)
    mixed = upsample(lifted, 2).reshape(lifted.shape[0], -1)
    mixed = (
        mixed
        + jnp.dot(w_skip, a0.reshape(a0.shape[0], -1), preferred_element_type=jnp.float32)
        + b_up[:, None]
    )
    hidden = jnp.maximum(mixed, 0.0).astype(jnp.bfloat16)
    logits = jnp.dot(w_out, hidden, preferred_element_type=jnp.float32) + b_out[:, None]
    return jax.nn.sigmoid(logits).reshape(1, 1, 3, E * E * E)


H = E // 2
REACH = 8
SLABS = H + 4
WIDE = E + 2 * REACH


def selections():
    row = jnp.arange(8 * SLABS)
    slab, kk = row // 8, row % 8
    offset = jnp.where(kk < 4, kk - 1, kk % 2)
    pick = 2 * (slab - 2) + offset + REACH
    rows = (pick[:, None] == jnp.arange(WIDE)[None, :]).astype(jnp.bfloat16)
    cell = jnp.arange(512)
    y, z = cell // E, cell % E
    to = ((y % 2) * 2 + z % 2) * 128 + (y // 2) * H + z // 2
    split = (to[:, None] == cell[None, :]).astype(jnp.bfloat16)
    return rows, split, split.T


def input_taps(w_in):
    table = [[-1] * 8 for _ in range(32)]
    for p in range(8):
        px, py, pz = p // 4, p // 2 % 2, p % 2
        same = py * 2 + pz
        other_y, other_z = (1 - py) * 2 + pz, py * 2 + 1 - pz
        table[same * 8 + px + 1][p] = 0
        table[same * 8 + px][p] = 1
        table[same * 8 + px + 2][p] = 2
        near_y, near_z = px + 1, px + 1
        far_y, far_z = 4 + px, 6 + px
        table[other_y * 8 + (far_y if py == 0 else near_y)][p] = 3
        table[other_y * 8 + (near_y if py == 0 else far_y)][p] = 4
        table[other_z * 8 + (far_z if pz == 0 else near_z)][p] = 5
        table[other_z * 8 + (near_z if pz == 0 else far_z)][p] = 6
    chans = w_in.shape[1]
    tap = jnp.repeat(jnp.array(table, jnp.int32), chans, axis=1)
    wide = jnp.tile(w_in[:, :, 0], (1, 8))
    total = jnp.zeros((32, 8 * chans), jnp.bfloat16)
    for t in range(7):
        total = jnp.where(tap == t, wide[t][None, :], total)
    return total


def three_terms(v):
    high = v.astype(jnp.bfloat16)
    rest = v - high.astype(jnp.float32)
    mid = rest.astype(jnp.bfloat16)
    low = (rest - mid.astype(jnp.float32)).astype(jnp.bfloat16)
    return high, mid, low


def block_kernel(
    s_ref, ex_ref, lo_ref, hi_ref, rows_ref, split_ref, join_ref, ctx_ref, below_ref, above_ref,
    w1_ref, b1_ref, wd_ref, bd_ref, wc_ref, wm_ref, bm_ref, wp_ref, bp_ref, wo_ref, bo_ref,
    out_ref,
    g_ref, p_ref, a0_ref, p1_ref, a1_ref, k1_ref, kd_ref, ku_ref, l_ref,
):
    bf, f32 = jnp.bfloat16, jnp.float32
    bx, by = s_ref[0], s_ref[1]
    first, last = s_ref[2] > 0, s_ref[3] > 0
    left, right = s_ref[4] > 0, s_ref[5] > 0

    def iota(shape, dim):
        return lax.broadcasted_iota(jnp.int32, shape, dim)

    def dot(a, b):
        return jnp.dot(a, b, preferred_element_type=f32)

    k1_ref[0:32, :] = w1_ref[...]
    k1_ref[32:48, :] = jnp.concatenate(
        [t.astype(f32) for t in three_terms(b1_ref[...])] + [jnp.zeros((13, 512), f32)], axis=0
    ).astype(bf)
    kd_ref[0:448, :] = wd_ref[...]
    kd_ref[448:512, :] = jnp.concatenate(
        [t.astype(f32) for t in three_terms(bd_ref[...])] + [jnp.zeros((61, 128), f32)], axis=0
    ).astype(bf)

    def near(dx, dy):
        x, y = bx + dx, by + dy
        ok = (x >= 0) & (x < 4) & (y >= 0) & (y < 4)
        x, y = jnp.clip(x, 0, 3), jnp.clip(y, 0, 3)
        v = ctx_ref[pl.ds(4 * x, 4), pl.ds(y, 1), :, :].reshape(64, 128)
        return jnp.where(ok, v, jnp.zeros_like(v))

    views = [near(0, 0), near(-1, 0), near(1, 0), near(0, -1), near(0, 1)]
    for other in (below_ref, above_ref):
        views.append(other[pl.ds(4 * bx, 4), pl.ds(by, 1), :, :].reshape(64, 128))
    total = dot(views[0], wc_ref[0])
    for t in range(1, 7):
        total = total + dot(views[t], wc_ref[t])
    terms = three_terms(total)
    bias = [t.astype(f32) for t in three_terms(bm_ref[...])]
    for q in range(4):
        ku_ref[q] = jnp.concatenate(
            [t[16 * q : 16 * q + 16].astype(f32) for t in terms] + bias + [jnp.zeros((77, 128), f32)],
            axis=0,
        ).astype(bf)

    field = jnp.concatenate([lo_ref[...], ex_ref[...], hi_ref[...]], axis=1)
    field = dot(rows_ref[...], field).astype(bf)
    for j in range(3):
        part = dot(field[:, 512 * j : 512 * j + 512], split_ref[...])
        for q in range(4):
            g_ref[q, :, 128 * j : 128 * j + 128] = part[:, 128 * q : 128 * q + 128]
    shape = (8 * SLABS, 384)
    kk = iota(shape, 0) % 8
    hz = iota(shape, 1) % H
    for q in range(4):
        py, pz = q // 2, q % 2
        v = g_ref[q]
        ys = pltpu.roll(v, H if py == 1 else 384 - H, axis=1)
        zs = pltpu.roll(v, 1 if pz == 1 else 383, axis=1)
        zs = jnp.where(hz == (0 if pz == 1 else H - 1), 0.0, zs)
        v = jnp.where(kk < 4, v, jnp.where(kk < 6, ys, zs))
        p_ref[:, 8 * q : 8 * q + 8, :] = v.reshape(SLABS, 8, 384)

    ones = jnp.where(iota((16, 384), 0) < 3, 1.0, 0.0)
    start = jnp.where(first, 0, 2)
    p1_ref[0:2] = jnp.zeros((2, 320, 128), bf)
    p1_ref[SLABS - 2 : SLABS] = jnp.zeros((2, 320, 128), bf)
    a1_ref[0] = jnp.zeros((288, 128), bf)
    a1_ref[H + 1] = jnp.zeros((288, 128), bf)

    def full_res(i, carry):
        s = start + i
        taps = jnp.concatenate([p_ref[s], ones], axis=0)
        taps = taps.T[32:352].astype(bf)
        pre = dot(taps, k1_ref[...])
        pool = jnp.maximum(
            jnp.maximum(pre[:, 0:128], pre[:, 128:256]), jnp.maximum(pre[:, 256:384], pre[:, 384:512])
        )
        pool = jnp.maximum(pool, pltpu.roll(pool, 64, axis=1))
        p1_ref[s] = jnp.maximum(pool, 0.0).astype(bf)

        @pl.when(jnp.logical_not(left))
        def _():
            p1_ref[s, 0:32] = jnp.zeros((32, 128), bf)

        @pl.when(jnp.logical_not(right))
        def _():
            p1_ref[s, 288:320] = jnp.zeros((32, 128), bf)

        @pl.when((s >= 2) & (s < H + 2))
        def _():
            a0_ref[s - 2] = jnp.maximum(pre[32:288], 0.0).astype(bf)

        return carry

    lax.fori_loop(0, H + 2, full_res, 0)

    lane = iota((288, 128), 1)
    zrow = iota((288, 128), 0) % H
    low = lane < 64
    cut = zrow == jnp.where(low, 0, H - 1)
    extra = jnp.where(lane < 67, 1.0, 0.0).astype(bf)
    begin = jnp.where(first, 0, 1)

    def half_res(i, carry):
        u = begin + i
        s = u + 1
        mid = p1_ref[s, 16:304]
        t1 = jnp.where(low, p1_ref[s - 1, 16:304], p1_ref[s + 1, 16:304])
        t2 = jnp.where(low, p1_ref[s, 0:288], p1_ref[s, 32:320])
        wide = mid.astype(f32)
        t3 = jnp.where(low, pltpu.roll(wide, 1, axis=0), pltpu.roll(wide, 287, axis=0))
        t3 = jnp.where(cut, 0.0, t3).astype(bf)
        t4 = jnp.where(low, mid, extra)
        pre = dot(jnp.concatenate([t1, t2], axis=1), kd_ref[0:256]) + dot(
            jnp.concatenate([t3, t4], axis=1), kd_ref[256:512]
        )
        a1_ref[u] = jnp.maximum(pre, 0.0).astype(bf)

        @pl.when(jnp.logical_not(left))
        def _():
            a1_ref[u, 0:16] = jnp.zeros((16, 128), bf)

        @pl.when(jnp.logical_not(right))
        def _():
            a1_ref[u, 272:288] = jnp.zeros((16, 128), bf)

        return carry

    lax.fori_loop(0, H + 1, half_res, 0)

    rows = iota((256, 128), 0)
    cols = iota((256, 128), 1)
    coarse = (rows // H) // 4 * 4 + rows % H // 4
    spread = jnp.where(cols < 48, jnp.where(cols % H == coarse, 1.0, 0.0), jnp.where(cols < 51, 1.0, 0.0))
    spread = spread.astype(bf)
    zfirst, zlast = rows % H == 0, rows % H == H - 1

    def decode(h, carry):
        u = h + 1
        mid = a1_ref[u, 16:272]
        wide = mid.astype(f32)
        zm = jnp.where(zfirst, 0.0, pltpu.roll(wide, 1, axis=0)).astype(bf)
        zp = jnp.where(zlast, 0.0, pltpu.roll(wide, 255, axis=0)).astype(bf)
        pre = dot(jnp.concatenate([a1_ref[u - 1, 16:272], a1_ref[u + 1, 16:272]], axis=1), wm_ref[0:256])
        pre = pre + dot(jnp.concatenate([a1_ref[u, 0:256], a1_ref[u, 32:288]], axis=1), wm_ref[256:512])
        pre = pre + dot(jnp.concatenate([zm, zp], axis=1), wm_ref[512:768])
        kc = jnp.concatenate([wm_ref[768:896], ku_ref[h // 4]], axis=0)
        pre = pre + dot(jnp.concatenate([mid, spread], axis=1), kc)
        a2 = jnp.maximum(pre, 0.0).astype(bf)
        logits = None
        for m in range(4):
            both = jnp.concatenate([a0_ref[h, :, 128 * m : 128 * m + 128], a2], axis=1)
            mixed = dot(both, wp_ref[...]) + bp_ref[...]
            hidden = jnp.maximum(mixed, 0.0).astype(bf)
            part = lax.dot_general(
                wo_ref[m], hidden, (((1,), (1,)), ((), ())), preferred_element_type=f32
            )
            logits = part if logits is None else logits + part
        logits = jax.nn.sigmoid(logits + bo_ref[...])
        for j in range(2):
            l_ref[j, pl.ds(pl.multiple_of(8 * h, 8), 8), :] = jnp.concatenate(
                [logits[8 * q : 8 * q + 8, 128 * j : 128 * j + 128] for q in range(4)], axis=1
            )
        return carry

    lax.fori_loop(0, H, decode, 0)

    for j in range(2):
        v = l_ref[j]
        high = v.astype(bf)
        rest = (v - high.astype(f32)).astype(bf)
        done = dot(high, join_ref[...]) + dot(rest, join_ref[...])
        for h in range(H):
            for px in range(2):
                at = (2 * h + px) * E * E + 512 * j
                out_ref[:, at : at + 512] = done[8 * h + 4 * px : 8 * h + 4 * px + 3]


def flat_shards(
    image,
    context,
    tissue,
    owner,
    neighbours,
    w_in,
    b_in,
    w_down,
    b_down,
    w_ctx,
    w_mid,
    b_mid,
    w_skip,
    w_lift,
    b_up,
    w_out,
    b_out,
):
    bf = jnp.bfloat16
    count = lax.axis_size("blk")
    half = count // 2
    nbr = neighbours[0, 0]
    me = lax.axis_index("blk")
    pos = jnp.sum(jnp.where(owner[0] == me, tissue[0], 0))
    have = (nbr >= 0).astype(jnp.int32)
    scalars = jnp.concatenate([jnp.stack([pos // 4, pos % 4]), have]).astype(jnp.int32)

    img = image.reshape(E, E * E)
    face = jnp.where(nbr[0] >= 0, img[:REACH], img[E - REACH :])
    face = lax.ppermute(face, "blk", [(i, (i + half) % count) for i in range(count)])
    zero = jnp.zeros_like(face)
    ex = jnp.concatenate(
        [jnp.where(nbr[0] >= 0, face, zero), img, jnp.where(nbr[1] >= 0, face, zero)], axis=0
    )
    ups = [(i, i + 1) for i in range(lax.axis_size("grp") - 1)]
    below = lax.ppermute(context, "grp", ups)
    above = lax.ppermute(context, "grp", [(j, i) for i, j in ups])
    lo = from_behind(ex[:, (E - REACH) * E :], "blk", 1)
    hi = from_behind(ex[:, : REACH * E], "blk", -1)
    lo = jnp.where(nbr[2] >= 0, lo, jnp.zeros_like(lo))
    hi = jnp.where(nbr[3] >= 0, hi, jnp.zeros_like(hi))

    rows, split, join = selections()
    c0, c1 = w_skip.shape[1], w_skip.shape[0]
    w1 = input_taps(w_in)
    b1 = jnp.tile(b_in, 8)[None, :]
    wd = jnp.swapaxes(w_down, 1, 2)
    wd = jnp.concatenate([wd[1:], wd[:1]], axis=0).reshape(7 * c0, c1)
    wm = jnp.swapaxes(w_mid, 1, 2)
    wm = jnp.concatenate([wm[1:], wm[:1]], axis=0).reshape(7 * c1, c1)
    skip, lift = w_skip.T, w_lift.T
    none = jnp.zeros_like(skip)
    wp = jnp.concatenate(
        [
            jnp.concatenate([skip, none], axis=1),
            jnp.concatenate([none, skip], axis=1),
            jnp.concatenate([lift, lift], axis=1),
        ],
        axis=0,
    )
    bp = jnp.tile(b_up, 2)[None, :]
    wo = jnp.zeros((4, 32, 2 * c1), bf)
    for m in range(4):
        px, py = m // 2, m % 2
        for pz in range(2):
            at = (py * 2 + pz) * 8 + px * 4
            wo = wo.at[m, at : at + 3, pz * c1 : (pz + 1) * c1].set(w_out)
    bo = jnp.tile(jnp.concatenate([b_out, jnp.zeros((1,), jnp.float32)]), 8)[:, None]

    grid4 = (16, 4, 16, context.shape[-1])
    vmem = pl.BlockSpec(memory_space=pltpu.VMEM)
    out = pl.pallas_call(
        block_kernel,
        out_shape=jax.ShapeDtypeStruct((3, E * E * E), jnp.float32),
        in_specs=[pl.BlockSpec(memory_space=pltpu.SMEM)] + [vmem] * 20,
        out_specs=vmem,
        scratch_shapes=[
            pltpu.VMEM((4, 8 * SLABS, 384), jnp.float32),
            pltpu.VMEM((SLABS, 32, 384), jnp.float32),
            pltpu.VMEM((H, 256, 512), bf),
            pltpu.VMEM((SLABS, 320, 128), bf),
            pltpu.VMEM((H + 2, 288, 128), bf),
            pltpu.VMEM((48, 512), bf),
            pltpu.VMEM((512, 128), bf),
            pltpu.VMEM((4, 128, 128), bf),
            pltpu.VMEM((2, 8 * H, 512), jnp.float32),
        ],
        compiler_params=pltpu.CompilerParams(vmem_limit_bytes=40 << 20),
    )(
        scalars, ex, lo, hi, rows, split, join,
        context.reshape(grid4), below.reshape(grid4), above.reshape(grid4),
        w1, b1, wd, b_down[None, :], w_ctx, wm, b_mid[None, :], wp, bp, wo, bo,
    )
    return out.reshape(1, 1, 3, E * E * E)


def solution(mesh):
    flat = mesh.shape["blk"] == 8
    return jax.shard_map(
        flat_shards if flat else layered_shards,
        mesh=mesh,
        in_specs=(
            P("grp", "blk", None),
            P("grp", None, None),
            P("grp", None),
            P("grp", None),
            P("grp", "blk", None),
            P(),
            P(),
            P(),
            P(),
            P(),
            P(),
            P(),
            P(),
            P(),
            P(),
            P(),
            P(),
        ),
        out_specs=P("grp", "blk", None, None),
        check_vma=False,
    )
```

```python
import jax
import jax.numpy as jnp
import numpy as np
from jax import lax
from jax.experimental import pallas as pl
from jax.experimental.pallas import tpu as pltpu
from jax.sharding import PartitionSpec as P

E = 32


def from_behind(shard, axis, by):
    devices = lax.axis_size(axis)
    return lax.ppermute(shard, axis, [(i, (i + by) % devices) for i in range(devices)])


def extended(shard, sides, width):
    for axis, dim in sides:
        devices, length = (lax.axis_size(axis), shard.shape[dim])
        up = [(i, (i + 1) % devices) for i in range(devices - 1)]
        down = [(j, i) for i, j in up]
        last = lax.slice_in_dim(shard, length - width, length, axis=dim)
        initial = lax.slice_in_dim(shard, 0, width, axis=dim)
        before = lax.ppermute(last, axis, up)
        after = lax.ppermute(initial, axis, down)
        shard = jnp.concatenate([before, shard, after], axis=dim)
    return shard


def faces_of(x):
    return jnp.stack([x[:, 0], x[:, -1], x[:, :, 0], x[:, :, -1], x[:, :, :, 0], x[:, :, :, -1]])


def conv_taps(x, halos, weight):
    chans = x.shape[0]
    views = [
        x,
        jnp.concatenate([halos[0][:, None], x[:, :-1]], 1),
        jnp.concatenate([x[:, 1:], halos[1][:, None]], 1),
        jnp.concatenate([halos[2][:, :, None], x[:, :, :-1]], 2),
        jnp.concatenate([x[:, :, 1:], halos[3][:, :, None]], 2),
        jnp.concatenate([halos[4][:, :, :, None], x[:, :, :, :-1]], 3),
        jnp.concatenate([x[:, :, :, 1:], halos[5][:, :, :, None]], 3),
    ]
    total = jnp.dot(weight[0], views[0].reshape(chans, -1), preferred_element_type=jnp.float32)
    for tap in range(1, 7):
        total = total + jnp.dot(
            weight[tap], views[tap].reshape(chans, -1), preferred_element_type=jnp.float32
        )
    return total


def upsample(v, factor):
    chans, side = (v.shape[0], v.shape[1])
    big = jnp.broadcast_to(
        v[:, :, None, :, None, :, None], (chans, side, factor, side, factor, side, factor)
    )
    return big.reshape(chans, side * factor, side * factor, side * factor)


def pooled(a0):
    half = a0.shape[1] // 2
    return a0.reshape(a0.shape[0], half, 2, half, 2, half, 2).max(axis=(2, 4, 6))


def neighbour_faces(x, nbr):
    flat = faces_of(x)
    count = lax.axis_size("blk")
    depth_blocks = count // 8
    offsets = [-(count // 2), count // 2, -depth_blocks, depth_blocks, -1, 1]
    pieces = []
    for direction in range(6):
        pieces.append(from_behind(flat[direction ^ 1], "blk", -offsets[direction]))
    mask = (nbr >= 0).astype(jnp.bfloat16)
    return jnp.stack(pieces) * mask[:, None, None, None]


def context_term(near, bx, by, bz, w_ctx, coarse, depth_blocks):
    side = 4 * coarse
    chans = near.shape[-1]
    regions = near.reshape(3, side, side, depth_blocks * coarse, chans)
    middle = jnp.pad(regions[1], ((coarse, coarse), (coarse, coarse), (0, 0), (0, 0)))
    zoff = bz * coarse
    xoff = bx * coarse
    yoff = by * coarse
    zero = jnp.zeros((), jnp.int32)
    size = (coarse, coarse, coarse, chans)
    shift = jnp.int32(coarse)
    taps = [
        lax.dynamic_slice(middle, (xoff + shift, yoff + shift, zoff, zero), size),
        lax.dynamic_slice(middle, (xoff, yoff + shift, zoff, zero), size),
        lax.dynamic_slice(middle, (xoff + 2 * shift, yoff + shift, zoff, zero), size),
        lax.dynamic_slice(middle, (xoff + shift, yoff, zoff, zero), size),
        lax.dynamic_slice(middle, (xoff + shift, yoff + 2 * shift, zoff, zero), size),
        lax.dynamic_slice(regions[0], (xoff, yoff, zoff, zero), size),
        lax.dynamic_slice(regions[2], (xoff, yoff, zoff, zero), size),
    ]
    total = jnp.dot(taps[0].reshape(-1, chans), w_ctx[0], preferred_element_type=jnp.float32)
    for tap in range(1, 7):
        total = total + jnp.dot(
            taps[tap].reshape(-1, chans), w_ctx[tap], preferred_element_type=jnp.float32
        )
    return total.T.reshape(-1, coarse, coarse, coarse)


def layered_shards(
    image,
    context,
    tissue,
    owner,
    neighbours,
    w_in,
    b_in,
    w_down,
    b_down,
    w_ctx,
    w_mid,
    b_mid,
    w_skip,
    w_lift,
    b_up,
    w_out,
    b_out,
):
    half = E // 2
    coarse = E // 8
    depth_blocks = tissue.shape[1] // 8
    nbr = neighbours[0, 0]
    volume = image.reshape(1, E, E, E)
    pre = conv_taps(volume, neighbour_faces(volume, nbr), w_in) + b_in[:, None]
    a0 = jnp.maximum(pre, 0.0).astype(jnp.bfloat16).reshape(-1, E, E, E)
    p1 = pooled(a0)
    pre = conv_taps(p1, neighbour_faces(p1, nbr), w_down) + b_down[:, None]
    a1 = jnp.maximum(pre, 0.0).astype(jnp.bfloat16).reshape(-1, half, half, half)
    me = lax.axis_index("blk")
    pos = jnp.sum(jnp.where(owner[0] == me, tissue[0], 0))
    bx = pos // (4 * depth_blocks)
    by = pos // depth_blocks % 4
    bz = pos % depth_blocks
    near = extended(context, (("grp", 0),), 1)
    cterm = context_term(near, bx, by, bz, w_ctx, coarse, depth_blocks)
    pre = conv_taps(a1, neighbour_faces(a1, nbr), w_mid) + b_mid[:, None]
    pre = pre + upsample(cterm, 4).reshape(cterm.shape[0], -1)
    a2 = jnp.maximum(pre, 0.0).astype(jnp.bfloat16)
    lifted = jnp.dot(w_lift, a2, preferred_element_type=jnp.float32).reshape(-1, half, half, half)
    mixed = upsample(lifted, 2).reshape(lifted.shape[0], -1)
    mixed = (
        mixed
        + jnp.dot(w_skip, a0.reshape(a0.shape[0], -1), preferred_element_type=jnp.float32)
        + b_up[:, None]
    )
    hidden = jnp.maximum(mixed, 0.0).astype(jnp.bfloat16)
    logits = jnp.dot(w_out, hidden, preferred_element_type=jnp.float32) + b_out[:, None]
    return jax.nn.sigmoid(logits).reshape(1, 1, 3, E * E * E)


H = E // 2
REACH = 8
SLABS = H + 4
WIDE = E + 2 * REACH


def selections():
    row = np.arange(8 * SLABS)
    slab, kk = row // 8, row % 8
    offset = np.where(kk < 4, kk - 1, kk % 2)
    shift = np.where(kk < 4, 0, np.where(kk < 6, WIDE, 2 * WIDE))
    pick = 2 * (slab - 2) + offset + REACH + shift
    rows = pick[:, None] == np.arange(3 * WIDE)[None, :]
    return jnp.asarray(rows, jnp.bfloat16)


def tap_table(chans):
    table = -np.ones((32, 8), np.int32)
    for p in range(8):
        px, py, pz = p // 4, p // 2 % 2, p % 2
        same = (py * 2 + pz) * 8
        other_y, other_z = ((1 - py) * 2 + pz) * 8, (py * 2 + 1 - pz) * 8
        near, far_y, far_z = px + 1, 4 + px, 6 + px
        table[same + near, p] = 0
        table[same + px, p] = 1
        table[same + px + 2, p] = 2
        table[other_y + (far_y if py == 0 else near), p] = 3
        table[other_y + (near if py == 0 else far_y), p] = 4
        table[other_z + (far_z if pz == 0 else near), p] = 5
        table[other_z + (near if pz == 0 else far_z), p] = 6
    return jnp.asarray(np.repeat(table, chans, axis=1))


def three_terms(v):
    high = v.astype(jnp.bfloat16)
    rest = v - high.astype(jnp.float32)
    mid = rest.astype(jnp.bfloat16)
    low = (rest - mid.astype(jnp.float32)).astype(jnp.bfloat16)
    return [t.astype(jnp.float32) for t in (high, mid, low)]


def block_kernel(
    tissue_ref, owner_ref, nbr_ref, bo_ref,
    ex_ref, lo_ref, hi_ref, rows_ref, ctx_ref, below_ref, above_ref,
    win_hbm, b1_hbm, wdown_hbm, bd_hbm, wc_hbm, wmid_hbm, bm_hbm, skip_hbm, lift_hbm, bp_hbm, wout_hbm, tap_hbm,
    out_ref,
    win_ref, b1_ref, wdown_ref, bd_ref, wc_ref, wmid_ref, bm_ref, skip_ref, lift_ref, bp_ref, wout_ref, tap_ref,
    sems, split_ref, p_ref, a0_ref, p1_ref, a1_ref, k1_ref, kd_ref, wm_ref, ku_ref, wp_ref, wo_ref, l_ref,
):
    bf, f32 = jnp.bfloat16, jnp.float32
    copies = [
        pltpu.make_async_copy(src, dst, sems.at[i])
        for i, (src, dst) in enumerate(
            (
                (win_hbm, win_ref), (b1_hbm, b1_ref), (wdown_hbm, wdown_ref), (bd_hbm, bd_ref), (wc_hbm, wc_ref),
                (wmid_hbm, wmid_ref), (bm_hbm, bm_ref), (skip_hbm, skip_ref), (lift_hbm, lift_ref),
                (bp_hbm, bp_ref), (wout_hbm, wout_ref), (tap_hbm, tap_ref),
            )
        )
    ]
    for copy in copies:
        copy.start()
    me = lax.axis_index("blk")
    pos = jnp.int32(0)
    for j in range(tissue_ref.shape[1]):
        pos = pos + jnp.where(owner_ref[0, j] == me, tissue_ref[0, j], 0)
    bx, by = pos // 4, pos % 4
    first = nbr_ref[0, 0] >= 0
    second = nbr_ref[0, 1] >= 0
    left, right = nbr_ref[0, 2] >= 0, nbr_ref[0, 3] >= 0

    def iota(shape, dim):
        return lax.broadcasted_iota(jnp.int32, shape, dim)

    def dot(a, b):
        return jnp.dot(a, b, preferred_element_type=f32)

    for part in range(4):
        cell = iota((128, 512), 0) + 128 * part
        y, z = cell // E, cell % E
        to = ((y % 2) * 2 + z % 2) * 128 + (y // 2) * H + z // 2
        split_ref[128 * part : 128 * part + 128, :] = jnp.where(to == iota((128, 512), 1), 1.0, 0.0).astype(bf)

    lo, hi = lo_ref[...].astype(f32), hi_ref[...].astype(f32)
    lo = jnp.where(left, lo, 0.0)
    hi = jnp.where(right, hi, 0.0)
    field = jnp.concatenate([lo, ex_ref[...].astype(f32), hi], axis=1)
    x = iota(field.shape, 0)
    field = jnp.where((x >= jnp.where(first, 0, REACH)) & (x < jnp.where(second, WIDE, WIDE - REACH)), field, 0.0)
    field = field.astype(bf)
    parts = [dot(field[:, 512 * j : 512 * j + 512], split_ref[...]) for j in range(3)]
    hz = iota((WIDE, 384), 1) % H
    for q in range(4):
        py, pz = q // 2, q % 2
        v = jnp.concatenate([part[:, 128 * q : 128 * q + 128] for part in parts], axis=1)
        ys = pltpu.roll(v, H if py == 1 else 384 - H, axis=1)
        zs = pltpu.roll(v, 1 if pz == 1 else 383, axis=1)
        zs = jnp.where(hz == (0 if pz == 1 else H - 1), 0.0, zs)
        v = dot(rows_ref[...], jnp.concatenate([v.astype(bf), ys.astype(bf), zs.astype(bf)], axis=0))
        p_ref[:, 8 * q : 8 * q + 8, :] = v.reshape(SLABS, 8, 384)

    for copy in copies:
        copy.wait()
    taps = jnp.concatenate([win_ref[...].astype(f32)] * 8, axis=1)
    tap = tap_ref[...]
    w1 = jnp.zeros(tap.shape, f32)
    for t in range(7):
        w1 = jnp.where(tap == t, taps[t : t + 1], w1)
    k1_ref[0:32, :] = w1.astype(bf)
    b1 = jnp.concatenate([b1_ref[...]] * 8, axis=1)
    k1_ref[32:48, :] = jnp.concatenate(three_terms(b1) + [jnp.zeros((13, 512), f32)], axis=0).astype(bf)
    kd_ref[0:384, :] = wdown_ref[1:7].reshape(384, 128)
    kd_ref[384:448, :] = wdown_ref[0]
    kd_ref[448:512, :] = jnp.concatenate(
        three_terms(bd_ref[...]) + [jnp.zeros((61, 128), f32)], axis=0
    ).astype(bf)
    for t in range(7):
        wm_ref[128 * t : 128 * t + 128, :] = wmid_ref[(t + 1) % 7].T
    skip, lift = skip_ref[...], lift_ref[...].T
    none = jnp.zeros_like(skip)
    wp_ref[0:64, :] = jnp.concatenate([skip, none], axis=1)
    wp_ref[64:128, :] = jnp.concatenate([none, skip], axis=1)
    wp_ref[128:256, :] = jnp.concatenate([lift, lift], axis=1)
    head = jnp.concatenate([wout_ref[...].astype(f32), jnp.zeros((1, 128), f32)], axis=0)
    head = jnp.concatenate([head] * 8, axis=0)
    group = iota((32, 128), 0) // 4
    for m in range(4):
        px, py = m // 2, m % 2
        wo_ref[m] = jnp.concatenate(
            [jnp.where(group == (py * 2 + pz) * 2 + px, head, 0.0) for pz in range(2)], axis=1
        ).astype(bf)
    chan = iota((32, 256), 0) % 4
    b_out = jnp.where(chan == 0, bo_ref[0], jnp.where(chan == 1, bo_ref[1], bo_ref[2]))

    def near(dx, dy):
        x, y = bx + dx, by + dy
        ok = (x >= 0) & (x < 4) & (y >= 0) & (y < 4)
        x, y = jnp.clip(x, 0, 3), jnp.clip(y, 0, 3)
        v = ctx_ref[pl.ds(4 * x, 4), pl.ds(y, 1), :, :].reshape(64, 128)
        return jnp.where(ok, v, jnp.zeros_like(v))

    views = [near(0, 0), near(-1, 0), near(1, 0), near(0, -1), near(0, 1)]
    for other in (below_ref, above_ref):
        views.append(other[pl.ds(4 * bx, 4), pl.ds(by, 1), :, :].reshape(64, 128))
    total = dot(views[0], wc_ref[0])
    for t in range(1, 7):
        total = total + dot(views[t], wc_ref[t])
    terms = three_terms(total)
    bias = three_terms(bm_ref[...])
    for q in range(4):
        ku_ref[q] = jnp.concatenate(
            [t[16 * q : 16 * q + 16] for t in terms] + bias + [jnp.zeros((77, 128), f32)], axis=0
        ).astype(bf)

    ones = jnp.where(iota((16, 384), 0) < 3, 1.0, 0.0)
    start = jnp.where(first, 0, 2)
    p1_ref[0:2] = jnp.zeros((2, 320, 128), bf)
    p1_ref[SLABS - 2 : SLABS] = jnp.zeros((2, 320, 128), bf)
    a1_ref[0] = jnp.zeros((288, 128), bf)
    a1_ref[H + 1] = jnp.zeros((288, 128), bf)

    def keep(ok, v):
        return jnp.where(ok, v, jnp.zeros_like(v))

    def full_res(i, carry):
        s = start + i
        taps = jnp.concatenate([p_ref[s], ones], axis=0)
        taps = taps.T[32:352].astype(bf)
        a0 = jnp.maximum(dot(taps, k1_ref[...]).astype(bf), jnp.zeros((), bf))
        a0_ref[s] = a0[32:288]
        pool = jnp.maximum(
            jnp.maximum(a0[:, 0:128], a0[:, 128:256]), jnp.maximum(a0[:, 256:384], a0[:, 384:512])
        )
        pool = jnp.maximum(pool, jnp.concatenate([pool[:, 64:128], pool[:, 0:64]], axis=1))
        p1_ref[s, 0:32] = keep(left, pool[0:32])
        p1_ref[s, 32:288] = pool[32:288]
        p1_ref[s, 288:320] = keep(right, pool[288:320])
        return carry

    lax.fori_loop(0, H + 2, full_res, 0, unroll=UNROLL[0])

    lane = iota((288, 128), 1)
    zrow = iota((288, 128), 0) % H
    low = lane < 64
    cut = zrow == jnp.where(low, 0, H - 1)
    extra = jnp.where(lane < 67, 1.0, 0.0).astype(bf)
    begin = jnp.where(first, 0, 1)

    def half_res(i, carry):
        u = begin + i
        s = u + 1
        mid = p1_ref[s, 16:304]
        t1 = jnp.where(low, p1_ref[s - 1, 16:304], p1_ref[s + 1, 16:304])
        t2 = jnp.where(low, p1_ref[s, 0:288], p1_ref[s, 32:320])
        wide = mid.astype(f32)
        t3 = jnp.where(low, pltpu.roll(wide, 1, axis=0), pltpu.roll(wide, 287, axis=0))
        t3 = jnp.where(cut, 0.0, t3).astype(bf)
        t4 = jnp.where(low, mid, extra)
        pre = dot(jnp.concatenate([t1, t2, t3, t4], axis=1), kd_ref[...])
        a1 = jnp.maximum(pre, 0.0).astype(bf)
        a1_ref[u, 0:16] = keep(left, a1[0:16])
        a1_ref[u, 16:272] = a1[16:272]
        a1_ref[u, 272:288] = keep(right, a1[272:288])
        return carry

    lax.fori_loop(0, H + 1, half_res, 0, unroll=UNROLL[1])

    rows = iota((256, 128), 0)
    cols = iota((256, 128), 1)
    coarse = (rows // H) // 4 * 4 + rows % H // 4
    spread = jnp.where(cols < 48, jnp.where(cols % H == coarse, 1.0, 0.0), jnp.where(cols < 51, 1.0, 0.0))
    spread = spread.astype(bf)
    zfirst, zlast = rows % H == 0, rows % H == H - 1

    def decode(h, carry):
        u = h + 1
        mid = a1_ref[u, 16:272]
        wide = mid.astype(f32)
        zm = jnp.where(zfirst, 0.0, pltpu.roll(wide, 1, axis=0)).astype(bf)
        zp = jnp.where(zlast, 0.0, pltpu.roll(wide, 255, axis=0)).astype(bf)
        field = jnp.concatenate(
            [a1_ref[u - 1, 16:272], a1_ref[u + 1, 16:272], a1_ref[u, 0:256], a1_ref[u, 32:288], zm, zp, mid, spread],
            axis=1,
        )
        pre = dot(field, jnp.concatenate([wm_ref[...], ku_ref[h // 4]], axis=0))
        a2 = jnp.maximum(pre, 0.0).astype(bf)
        logits = None
        b_up = jnp.concatenate([bp_ref[...]] * 2, axis=1)
        for m in range(4):
            both = jnp.concatenate([a0_ref[h + 2, :, 128 * m : 128 * m + 128], a2], axis=1)
            hidden = jnp.maximum((dot(both, wp_ref[...]) + b_up).astype(bf), jnp.zeros((), bf))
            part = lax.dot_general(
                wo_ref[m], hidden, (((1,), (1,)), ((), ())), preferred_element_type=f32
            )
            logits = part if logits is None else logits + part
        logits = jax.nn.sigmoid(logits + b_out)
        for j in range(2):
            for q in range(4):
                l_ref[j, q, pl.ds(pl.multiple_of(8 * h, 8), 8), :] = logits[
                    8 * q : 8 * q + 8, 128 * j : 128 * j + 128
                ]
        return carry

    lax.fori_loop(0, H, decode, 0, unroll=UNROLL[2])

    v = jnp.concatenate(
        [
            jnp.concatenate([l_ref[j, q, pl.ds(c, E, stride=4), :] for q in range(4)], axis=1)
            for j in range(2)
            for c in range(3)
        ],
        axis=0,
    )
    high = v.astype(bf)
    rest = (v - high.astype(f32)).astype(bf)

    def back(t):
        return lax.dot_general(t, split_ref[...], (((1,), (1,)), ((), ())), preferred_element_type=f32)

    done = back(high) + back(rest)
    for j in range(2):
        for c in range(3):
            at = E * (3 * j + c)
            for b in range(4):
                out_ref[pl.ds(256 * c + 4 * j + b, E, stride=8), :] = done[at : at + E, 128 * b : 128 * b + 128]


UNROLL = (2, 1, 2)


def flat_shards(
    image,
    context,
    tissue,
    owner,
    neighbours,
    w_in,
    b_in,
    w_down,
    b_down,
    w_ctx,
    w_mid,
    b_mid,
    w_skip,
    w_lift,
    b_up,
    w_out,
    b_out,
):
    bf = jnp.bfloat16
    count = lax.axis_size("blk")
    half = count // 2
    img = image.reshape(E, E * E)
    face = jnp.concatenate([img[E - REACH :], img[:REACH]], axis=0)
    face = lax.ppermute(face, "blk", [(i, (i + half) % count) for i in range(count)])
    ex = jnp.concatenate([face[:REACH], img, face[REACH:]], axis=0)
    lo = from_behind(ex[:, (E - REACH) * E :], "blk", 1)
    hi = from_behind(ex[:, : REACH * E], "blk", -1)
    ups = [(i, i + 1) for i in range(lax.axis_size("grp") - 1)]
    below = lax.ppermute(context, "grp", ups)
    above = lax.ppermute(context, "grp", [(j, i) for i, j in ups])

    rows = selections()
    grid4 = (16, 4, 16, context.shape[-1])
    vmem = pl.BlockSpec(memory_space=pltpu.VMEM)
    smem = pl.BlockSpec(memory_space=pltpu.SMEM)
    operands = (
        tissue, owner, neighbours[0], b_out,
        ex, lo, hi, rows,
        context.reshape(grid4), below.reshape(grid4), above.reshape(grid4),
        w_in[:, :, 0], b_in[None, :], jnp.swapaxes(w_down, 1, 2), b_down[None, :],
        w_ctx, w_mid, b_mid[None, :], w_skip.T, w_lift, b_up[None, :], w_out, tap_table(w_in.shape[1]),
    )
    held = operands[11:]
    out = pl.pallas_call(
        block_kernel,
        out_shape=jax.ShapeDtypeStruct((3 * E * E * E // 128, 128), jnp.float32),
        in_specs=[smem] * 4 + [vmem] * 7 + [pl.BlockSpec(memory_space=pltpu.HBM)] * len(held),
        out_specs=vmem,
        scratch_shapes=[pltpu.VMEM(v.shape, v.dtype) for v in held]
        + [
            pltpu.SemaphoreType.DMA((len(held),)),
            pltpu.VMEM((512, 512), bf),
            pltpu.VMEM((SLABS, 32, 384), jnp.float32),
            pltpu.VMEM((SLABS, 256, 512), bf),
            pltpu.VMEM((SLABS, 320, 128), bf),
            pltpu.VMEM((H + 2, 288, 128), bf),
            pltpu.VMEM((48, 512), bf),
            pltpu.VMEM((512, 128), bf),
            pltpu.VMEM((896, 128), bf),
            pltpu.VMEM((4, 128, 128), bf),
            pltpu.VMEM((256, 256), bf),
            pltpu.VMEM((4, 32, 256), bf),
            pltpu.VMEM((2, 4, 8 * H, 128), jnp.float32),
        ],
        compiler_params=pltpu.CompilerParams(vmem_limit_bytes=67043328),
    )(*operands)
    return out.reshape(1, 1, 3, E * E * E)


def solution(mesh):
    flat = mesh.shape["blk"] == 8
    return jax.shard_map(
        flat_shards if flat else layered_shards,
        mesh=mesh,
        in_specs=(
            P("grp", "blk", None),
            P("grp", None, None),
            P("grp", None),
            P("grp", None),
            P("grp", "blk", None),
            P(),
            P(),
            P(),
            P(),
            P(),
            P(),
            P(),
            P(),
            P(),
            P(),
            P(),
            P(),
        ),
        out_specs=P("grp", "blk", None, None),
        check_vma=False,
    )
```

```python
import jax
import jax.numpy as jnp
import numpy as np
from jax import lax
from jax.experimental import pallas as pl
from jax.experimental.pallas import tpu as pltpu
from jax.sharding import PartitionSpec as P


E = 32


def from_behind(shard, axis, by):
    devices = lax.axis_size(axis)
    return lax.ppermute(shard, axis, [(i, (i + by) % devices) for i in range(devices)])


def extended(shard, sides, width):
    for axis, dim in sides:
        devices, length = (lax.axis_size(axis), shard.shape[dim])
        up = [(i, (i + 1) % devices) for i in range(devices - 1)]
        down = [(j, i) for i, j in up]
        last = lax.slice_in_dim(shard, length - width, length, axis=dim)
        initial = lax.slice_in_dim(shard, 0, width, axis=dim)
        before = lax.ppermute(last, axis, up)
        after = lax.ppermute(initial, axis, down)
        shard = jnp.concatenate([before, shard, after], axis=dim)
    return shard


def faces_of(x):
    return jnp.stack([x[:, 0], x[:, -1], x[:, :, 0], x[:, :, -1], x[:, :, :, 0], x[:, :, :, -1]])


def conv_taps(x, halos, weight):
    chans = x.shape[0]
    views = [
        x,
        jnp.concatenate([halos[0][:, None], x[:, :-1]], 1),
        jnp.concatenate([x[:, 1:], halos[1][:, None]], 1),
        jnp.concatenate([halos[2][:, :, None], x[:, :, :-1]], 2),
        jnp.concatenate([x[:, :, 1:], halos[3][:, :, None]], 2),
        jnp.concatenate([halos[4][:, :, :, None], x[:, :, :, :-1]], 3),
        jnp.concatenate([x[:, :, :, 1:], halos[5][:, :, :, None]], 3),
    ]
    total = jnp.dot(weight[0], views[0].reshape(chans, -1), preferred_element_type=jnp.float32)
    for tap in range(1, 7):
        total = total + jnp.dot(
            weight[tap], views[tap].reshape(chans, -1), preferred_element_type=jnp.float32
        )
    return total


def upsample(v, factor):
    chans, side = (v.shape[0], v.shape[1])
    big = jnp.broadcast_to(
        v[:, :, None, :, None, :, None], (chans, side, factor, side, factor, side, factor)
    )
    return big.reshape(chans, side * factor, side * factor, side * factor)


def pooled(a0):
    half = a0.shape[1] // 2
    return a0.reshape(a0.shape[0], half, 2, half, 2, half, 2).max(axis=(2, 4, 6))


def neighbour_faces(x, nbr):
    flat = faces_of(x)
    count = lax.axis_size("blk")
    depth_blocks = count // 8
    offsets = [-(count // 2), count // 2, -depth_blocks, depth_blocks, -1, 1]
    pieces = []
    for direction in range(6):
        pieces.append(from_behind(flat[direction ^ 1], "blk", -offsets[direction]))
    mask = (nbr >= 0).astype(jnp.bfloat16)
    return jnp.stack(pieces) * mask[:, None, None, None]


def context_term(near, bx, by, bz, w_ctx, coarse, depth_blocks):
    side = 4 * coarse
    chans = near.shape[-1]
    regions = near.reshape(3, side, side, depth_blocks * coarse, chans)
    middle = jnp.pad(regions[1], ((coarse, coarse), (coarse, coarse), (0, 0), (0, 0)))
    zoff = bz * coarse
    xoff = bx * coarse
    yoff = by * coarse
    zero = jnp.zeros((), jnp.int32)
    size = (coarse, coarse, coarse, chans)
    shift = jnp.int32(coarse)
    taps = [
        lax.dynamic_slice(middle, (xoff + shift, yoff + shift, zoff, zero), size),
        lax.dynamic_slice(middle, (xoff, yoff + shift, zoff, zero), size),
        lax.dynamic_slice(middle, (xoff + 2 * shift, yoff + shift, zoff, zero), size),
        lax.dynamic_slice(middle, (xoff + shift, yoff, zoff, zero), size),
        lax.dynamic_slice(middle, (xoff + shift, yoff + 2 * shift, zoff, zero), size),
        lax.dynamic_slice(regions[0], (xoff, yoff, zoff, zero), size),
        lax.dynamic_slice(regions[2], (xoff, yoff, zoff, zero), size),
    ]
    total = jnp.dot(taps[0].reshape(-1, chans), w_ctx[0], preferred_element_type=jnp.float32)
    for tap in range(1, 7):
        total = total + jnp.dot(
            taps[tap].reshape(-1, chans), w_ctx[tap], preferred_element_type=jnp.float32
        )
    return total.T.reshape(-1, coarse, coarse, coarse)


def layered_shards(
    image,
    context,
    tissue,
    owner,
    neighbours,
    w_in,
    b_in,
    w_down,
    b_down,
    w_ctx,
    w_mid,
    b_mid,
    w_skip,
    w_lift,
    b_up,
    w_out,
    b_out,
):
    half = E // 2
    coarse = E // 8
    depth_blocks = tissue.shape[1] // 8
    nbr = neighbours[0, 0]
    volume = image.reshape(1, E, E, E)
    pre = conv_taps(volume, neighbour_faces(volume, nbr), w_in) + b_in[:, None]
    a0 = jnp.maximum(pre, 0.0).astype(jnp.bfloat16).reshape(-1, E, E, E)
    p1 = pooled(a0)
    pre = conv_taps(p1, neighbour_faces(p1, nbr), w_down) + b_down[:, None]
    a1 = jnp.maximum(pre, 0.0).astype(jnp.bfloat16).reshape(-1, half, half, half)
    me = lax.axis_index("blk")
    pos = jnp.sum(jnp.where(owner[0] == me, tissue[0], 0))
    bx = pos // (4 * depth_blocks)
    by = pos // depth_blocks % 4
    bz = pos % depth_blocks
    near = extended(context, (("grp", 0),), 1)
    cterm = context_term(near, bx, by, bz, w_ctx, coarse, depth_blocks)
    pre = conv_taps(a1, neighbour_faces(a1, nbr), w_mid) + b_mid[:, None]
    pre = pre + upsample(cterm, 4).reshape(cterm.shape[0], -1)
    a2 = jnp.maximum(pre, 0.0).astype(jnp.bfloat16)
    lifted = jnp.dot(w_lift, a2, preferred_element_type=jnp.float32).reshape(-1, half, half, half)
    mixed = upsample(lifted, 2).reshape(lifted.shape[0], -1)
    mixed = (
        mixed
        + jnp.dot(w_skip, a0.reshape(a0.shape[0], -1), preferred_element_type=jnp.float32)
        + b_up[:, None]
    )
    hidden = jnp.maximum(mixed, 0.0).astype(jnp.bfloat16)
    logits = jnp.dot(w_out, hidden, preferred_element_type=jnp.float32) + b_out[:, None]
    return jax.nn.sigmoid(logits).reshape(1, 1, 3, E * E * E)


H = E // 2
REACH = 8
SLABS = H + 4
WIDE = E + 2 * REACH


def selections():
    row = np.arange(8 * SLABS)
    slab, kk = row // 8, row % 8
    offset = np.where(kk < 4, kk - 1, kk % 2)
    shift = np.where(kk < 4, 0, np.where(kk < 6, WIDE, 2 * WIDE))
    pick = 2 * (slab - 2) + offset + REACH + shift
    rows = pick[:, None] == np.arange(3 * WIDE)[None, :]
    return jnp.asarray(rows, jnp.bfloat16)


def tap_table(chans):
    table = -np.ones((32, 8), np.int32)
    for p in range(8):
        px, py, pz = p // 4, p // 2 % 2, p % 2
        same = (py * 2 + pz) * 8
        other_y, other_z = ((1 - py) * 2 + pz) * 8, (py * 2 + 1 - pz) * 8
        near, far_y, far_z = px + 1, 4 + px, 6 + px
        table[same + near, p] = 0
        table[same + px, p] = 1
        table[same + px + 2, p] = 2
        table[other_y + (far_y if py == 0 else near), p] = 3
        table[other_y + (near if py == 0 else far_y), p] = 4
        table[other_z + (far_z if pz == 0 else near), p] = 5
        table[other_z + (near if pz == 0 else far_z), p] = 6
    return jnp.asarray(np.repeat(table, chans, axis=1))


def three_terms(v):
    high = v.astype(jnp.bfloat16)
    rest = v - high.astype(jnp.float32)
    mid = rest.astype(jnp.bfloat16)
    low = (rest - mid.astype(jnp.float32)).astype(jnp.bfloat16)
    return [t.astype(jnp.float32) for t in (high, mid, low)]


def block_kernel(
    tissue_ref, owner_ref, nbr_ref, bo_ref,
    img_ref, other_ref, lo_ref, hi_ref, rows_ref, ctx_hbm, even_hbm, odd_hbm,
    win_hbm, b1_hbm, wdown_hbm, bd_hbm, wc_hbm, wmid_hbm, bm_hbm, skip_hbm, lift_hbm, bp_hbm, wout_hbm, tap_hbm,
    out_ref,
    win_ref, b1_ref, wdown_ref, bd_ref, wc_ref, wmid_ref, bm_ref, skip_ref, lift_ref, bp_ref, wout_ref, tap_ref,
    view_ref, view_sems, sems, split_ref, p_ref, a0_ref, p1_ref, a1_ref, k1_ref, kd_ref, wm_ref, ku_ref, wp_ref, wo_ref, l_ref, bup_ref, spread_ref,
):
    bf, f32 = jnp.bfloat16, jnp.float32
    copies = [
        pltpu.make_async_copy(src, dst, sems.at[i])
        for i, (src, dst) in enumerate(
            (
                (win_hbm, win_ref), (b1_hbm, b1_ref), (wdown_hbm, wdown_ref), (bd_hbm, bd_ref), (wc_hbm, wc_ref),
                (wmid_hbm, wmid_ref), (bm_hbm, bm_ref), (skip_hbm, skip_ref), (lift_hbm, lift_ref),
                (bp_hbm, bp_ref), (wout_hbm, wout_ref), (tap_hbm, tap_ref),
            )
        )
    ]
    for copy in copies:
        copy.start()
    me = lax.axis_index("blk")
    pos = jnp.int32(0)
    for j in range(tissue_ref.shape[1]):
        pos = pos + jnp.where(owner_ref[0, j] == me, tissue_ref[0, j], 0)
    bx, by = pos // 4, pos % 4
    oks = []
    for t, (dx, dy) in enumerate(((0, 0), (-1, 0), (1, 0), (0, -1), (0, 1), (0, 0), (0, 0))):
        x, y = bx + dx, by + dy
        oks.append((x >= 0) & (x < 4) & (y >= 0) & (y < 4) if dx or dy else None)
        x, y = jnp.clip(x, 0, 3), jnp.clip(y, 0, 3)
        source = ctx_hbm if t < 5 else (even_hbm, odd_hbm)[t - 5]
        copies.append(
            pltpu.make_async_copy(source.at[pl.ds(4 * x, 4), pl.ds(y, 1)], view_ref.at[t], view_sems.at[t])
        )
        copies[-1].start()
    first = nbr_ref[0, 0] >= 0
    second = nbr_ref[0, 1] >= 0
    left, right = nbr_ref[0, 2] >= 0, nbr_ref[0, 3] >= 0

    def iota(shape, dim):
        return lax.broadcasted_iota(jnp.int32, shape, dim)

    def dot(a, b):
        return jnp.dot(a, b, preferred_element_type=f32)

    cell = iota((512, 1), 0)
    y, z = cell >> 5, cell & (E - 1)
    to = ((y & 1) * 2 + (z & 1)) * 128 + (y >> 1) * H + (z >> 1)
    for part in range(4):
        at = slice(128 * part, 128 * part + 128)
        split_ref[at, :] = jnp.where(to[at] == iota((128, 512), 1), 1.0, 0.0).astype(bf)

    lo, hi = lo_ref[...].astype(f32), hi_ref[...].astype(f32)
    lo = jnp.where(left, lo, 0.0)
    hi = jnp.where(right, hi, 0.0)
    none = jnp.zeros_like(lo)
    other = other_ref[...].astype(f32)
    mid = jnp.concatenate([other[E - REACH :], img_ref[...].astype(f32), other[:REACH]], axis=0)
    field = jnp.concatenate([none, lo, mid, hi, none], axis=1)
    x = iota(field.shape, 0)
    field = jnp.where((x >= jnp.where(first, 0, REACH)) & (x < jnp.where(second, WIDE, WIDE - REACH)), field, 0.0)
    field = field.astype(bf)
    parts = [dot(field[:, 512 * j : 512 * j + 512], split_ref[...]) for j in range(4)]
    hz = iota((WIDE, 512), 1) & (H - 1)
    inner = iota((8 * SLABS, 128), 1) < 64
    for q in range(4):
        py, pz = q // 2, q % 2
        v = jnp.concatenate([part[:, 128 * q : 128 * q + 128] for part in parts], axis=1)
        ys = pltpu.roll(v, H if py == 1 else 512 - H, axis=1)
        zs = pltpu.roll(v, 1 if pz == 1 else 511, axis=1)
        zs = jnp.where(hz == (0 if pz == 1 else H - 1), 0.0, zs)
        v = dot(rows_ref[...], jnp.concatenate([v.astype(bf), ys.astype(bf), zs.astype(bf)], axis=0))
        p_ref[:, 8 * q : 8 * q + 8, 0:256] = v[:, 128:384].reshape(SLABS, 8, 256)
        edge = jnp.where(inner, v[:, 384:512], v[:, 0:128])
        p_ref[:, 8 * q : 8 * q + 8, 256:384] = edge.reshape(SLABS, 8, 128)

    for copy in copies:
        copy.wait()
    taps = jnp.concatenate([win_ref[...].astype(f32)] * 8, axis=1)
    tap = tap_ref[...]
    w1 = jnp.zeros(tap.shape, f32)
    for t in range(7):
        w1 = jnp.where(tap == t, taps[t : t + 1], w1)
    b1 = jnp.concatenate([b1_ref[...]] * 8, axis=1)
    k1_ref[...] = jnp.concatenate([w1] + three_terms(b1) + [jnp.zeros((13, 512), f32)], axis=0).T.astype(bf)
    for j, pair in enumerate(((1, 2), (3, 4), (5, 6), (0, None))):
        upper = wdown_ref[pair[0]].astype(f32)
        if pair[1] is None:
            lower = jnp.concatenate(three_terms(bd_ref[...]) + [jnp.zeros((61, 128), f32)], axis=0)
        else:
            lower = wdown_ref[pair[1]].astype(f32)
        kd_ref[:, 128 * j : 128 * j + 128] = jnp.concatenate([upper, lower], axis=0).T.astype(bf)
    for t in range(7):
        wm_ref[:, 128 * t : 128 * t + 128] = wmid_ref[(t + 1) % 7]
    skip = skip_ref[...].astype(f32).T
    skip = jnp.concatenate([skip, jnp.zeros_like(skip)], axis=1)
    wp_ref[0:128, 0:128] = skip.astype(bf)
    wp_ref[128:256, 0:128] = pltpu.roll(skip, 64, axis=1).astype(bf)
    wp_ref[0:128, 128:256] = lift_ref[...]
    wp_ref[128:256, 128:256] = lift_ref[...]
    bup_ref[...] = jnp.broadcast_to(bp_ref[...], (128, 128)).T
    head = jnp.concatenate([wout_ref[...].astype(f32), jnp.zeros((1, 128), f32)], axis=0)
    head = jnp.concatenate([head] * 8, axis=0)
    group = iota((32, 128), 0) >> 2
    for m in range(4):
        px, py = m // 2, m % 2
        wo_ref[:, 256 * m : 256 * m + 256] = jnp.concatenate(
            [jnp.where(group == (py * 2 + pz) * 2 + px, head, 0.0) for pz in range(2)], axis=1
        ).astype(bf)
    chan = iota((32, 256), 0) & 3
    b_out = jnp.where(chan == 0, bo_ref[0], jnp.where(chan == 1, bo_ref[1], bo_ref[2]))

    views = []
    for t in range(7):
        v = view_ref[t].reshape(64, 128)
        views.append(v if oks[t] is None else jnp.where(oks[t], v, jnp.zeros_like(v)))
    total = dot(views[0], wc_ref[0])
    for t in range(1, 5):
        total = total + dot(views[t], wc_ref[t])
    odd = lax.axis_index("grp") % 2
    total = total + dot(views[5], wc_ref[6 - odd]) + dot(views[6], wc_ref[5 + odd])
    terms = three_terms(total)
    bias = three_terms(bm_ref[...])
    for q in range(4):
        ku_ref[q] = jnp.concatenate(
            [t[16 * q : 16 * q + 16] for t in terms] + bias + [jnp.zeros((77, 128), f32)], axis=0
        ).T.astype(bf)

    ones = jnp.where(iota((16, 384), 0) < 3, 1.0, 0.0)
    near_x, next_x = jnp.where(first, 1, H + 2), jnp.where(first, 0, H + 3)
    zero = jnp.zeros((), bf)

    def keep(ok, v):
        return jnp.where(ok, v, jnp.zeros_like(v))

    def full_res(i):
        slabs = (2 * i, 2 * i + 1)
        at = (near_x, next_x) if 2 * i == H else (2 * i + 2, 2 * i + 3)
        taps = [jnp.concatenate([p_ref[s], ones], axis=0).astype(bf) for s in at]
        taps = jnp.concatenate([t[:, 0:256] for t in taps] + [t[:, 256:384] for t in taps], axis=1)
        a0 = jnp.maximum(dot(k1_ref[...], taps).astype(bf), zero)
        pool = a0[0:64]
        for p in range(1, 8):
            pool = jnp.maximum(pool, a0[64 * p : 64 * p + 64])
        for k, s in enumerate(slabs):
            if s < H:
                a0_ref[s] = a0[:, 256 * k : 256 * k + 256]
            edge = pool[:, 512 + 128 * k : 640 + 128 * k]
            p1_ref[s, :, 0:128] = keep(left, edge)
            p1_ref[s, :, 128:384] = pool[:, 256 * k : 256 * k + 256]
            p1_ref[s, :, 384:512] = keep(right, edge)

    def beside(ref, s, lanes):
        if 0 < s < H - 1:
            return ref[s - 1, :, lanes], ref[s + 1, :, lanes]
        if s == 0:
            return keep(first, ref[H, :, lanes]), ref[1, :, lanes]
        if s == H - 1:
            return ref[H - 2, :, lanes], keep(second, ref[H, :, lanes])
        behind, inside = ref[H + 1, :, lanes], jnp.where(first, ref[0, :, lanes], ref[H - 1, :, lanes])
        return jnp.where(first, behind, inside), jnp.where(first, inside, behind)

    hz = iota((64, 512), 1) & (H - 1)
    notfirst = jnp.where(hz == 0, 0.0, 1.0).astype(bf)
    notlast = jnp.where(hz == H - 1, 0.0, 1.0).astype(bf)
    extra = jnp.where(iota((64, 512), 0) < 3, 1.0, 0.0).astype(bf)

    def half_res(s):
        mid = p1_ref[s]
        field = jnp.concatenate(
            [
                *beside(p1_ref, s, slice(0, 512)), pltpu.roll(mid, H, axis=1), pltpu.roll(mid, 512 - H, axis=1),
                pltpu.roll(mid, 1, axis=1) * notfirst, pltpu.roll(mid, 511, axis=1) * notlast, mid, extra,
            ],
            axis=0,
        )
        a1 = jnp.maximum(dot(kd_ref[...], field).astype(bf), zero)
        a1_ref[s, :, 0:128] = keep(left, a1[:, 0:128])
        a1_ref[s, :, 128:384] = a1[:, 128:384]
        a1_ref[s, :, 384:512] = keep(right, a1[:, 384:512])

    rows = iota((128, 256), 0)
    cols = iota((128, 256), 1)
    coarse = (cols >> 6) * 4 + ((cols & (H - 1)) >> 2)
    spread = jnp.where(rows < 48, jnp.where((rows & (H - 1)) == coarse, 1.0, 0.0), jnp.where(rows < 51, 1.0, 0.0))
    spread_ref[...] = spread.astype(bf)
    hz = cols & (H - 1)
    notfirst2 = jnp.where(hz == 0, 0.0, 1.0).astype(bf)
    notlast2 = jnp.where(hz == H - 1, 0.0, 1.0).astype(bf)

    def decode(h):
        wide = a1_ref[h]
        mid = wide[:, 128:384]
        field = jnp.concatenate(
            [
                *beside(a1_ref, h, slice(128, 384)),
                pltpu.roll(wide, H, axis=1)[:, 128:384], pltpu.roll(wide, 512 - H, axis=1)[:, 128:384],
                pltpu.roll(mid, 1, axis=1) * notfirst2, pltpu.roll(mid, 255, axis=1) * notlast2, mid, spread_ref[...],
            ],
            axis=0,
        )
        pre = dot(jnp.concatenate([wm_ref[...], ku_ref[h // 4]], axis=1), field)
        a2 = jnp.maximum(pre.astype(bf), zero)
        b_up = bup_ref[...]
        b_up = jnp.concatenate([b_up, b_up], axis=1)
        b_up = jnp.concatenate([b_up, b_up], axis=0)
        hidden = []
        for m in range(4):
            both = jnp.concatenate([a0_ref[h, 128 * m : 128 * m + 128, :], a2], axis=0)
            hidden.append(jnp.maximum((dot(wp_ref[...], both) + b_up).astype(bf), zero))
        logits = dot(wo_ref[...], jnp.concatenate(hidden, axis=0))
        logits = jax.nn.sigmoid(logits + b_out)
        for j in range(2):
            for q in range(4):
                l_ref[j, q, 8 * h : 8 * h + 8, :] = logits[
                    8 * q : 8 * q + 8, 128 * j : 128 * j + 128
                ]

    for stage, index in ORDER:
        (full_res, half_res, decode)[stage](index)

    v = jnp.concatenate(
        [
            jnp.concatenate([l_ref[j, q, pl.ds(c, E, stride=4), :] for q in range(4)], axis=1)
            for j in range(2)
            for c in range(3)
        ],
        axis=0,
    )
    high = v.astype(bf)
    rest = (v - high.astype(f32)).astype(bf)

    def back(t):
        return lax.dot_general(t, split_ref[...], (((1,), (1,)), ((), ())), preferred_element_type=f32)

    done = back(high) + back(rest)
    for j in range(2):
        for c in range(3):
            at = E * (3 * j + c)
            for b in range(4):
                out_ref[pl.ds(256 * c + 4 * j + b, E, stride=8), :] = done[at : at + E, 128 * b : 128 * b + 128]


ORDER = (
    [(0, H // 2)] + [(0, i) for i in range(H // 2)] + [(1, H)] + [(1, s) for s in range(H)] + [(2, h) for h in range(H)]
)


def flat_shards(
    image,
    context,
    tissue,
    owner,
    neighbours,
    w_in,
    b_in,
    w_down,
    b_down,
    w_ctx,
    w_mid,
    b_mid,
    w_skip,
    w_lift,
    b_up,
    w_out,
    b_out,
):
    bf = jnp.bfloat16
    count = lax.axis_size("blk")
    half = count // 2
    img = image.reshape(E, E * E)
    other = lax.ppermute(img, "blk", [(i, (i + half) % count) for i in range(count)])
    grp = lax.axis_size("grp")
    pairs = [[pair for i in range(odd, grp - 1, 2) for pair in ((i, i + 1), (i + 1, i))] for odd in range(2)]
    swaps = [lax.ppermute(context, "grp", pair) for pair in pairs]

    def face(mid, side, lanes):
        return jnp.concatenate([side[E - REACH :, lanes], mid[:, lanes], side[:REACH, lanes]], axis=0)

    def turn(shard, by):
        return lax.ppermute(shard, "blk", [(i, i // half * half + (i + by) % half) for i in range(count)])

    high, low = slice((E - REACH) * E, E * E), slice(0, REACH * E)
    place = lax.axis_index("blk") % half
    lo = turn(jnp.where(place == half - 1, face(other, img, high), face(img, other, high)), 1)
    hi = turn(jnp.where(place == 0, face(other, img, low), face(img, other, low)), -1)

    rows = selections()
    grid4 = (16, 4, 16, context.shape[-1])
    vmem = pl.BlockSpec(memory_space=pltpu.VMEM)
    smem = pl.BlockSpec(memory_space=pltpu.SMEM)
    operands = (
        tissue, owner, neighbours[0], b_out,
        img, other, lo, hi, rows,
        context.reshape(grid4), swaps[0].reshape(grid4), swaps[1].reshape(grid4),
        w_in[:, :, 0], b_in[None, :], jnp.swapaxes(w_down, 1, 2), b_down[None, :],
        w_ctx, w_mid, b_mid[None, :], w_skip.T, w_lift, b_up[None, :], w_out, tap_table(w_in.shape[1]),
    )
    held = operands[12:]
    out = pl.pallas_call(
        block_kernel,
        out_shape=jax.ShapeDtypeStruct((3 * E * E * E // 128, 128), jnp.float32),
        in_specs=[smem] * 4 + [vmem] * 5 + [pl.BlockSpec(memory_space=pltpu.HBM)] * (3 + len(held)),
        out_specs=vmem,
        scratch_shapes=[pltpu.VMEM(v.shape, v.dtype) for v in held]
        + [
            pltpu.VMEM((7, 4, 1, 16, context.shape[-1]), bf),
            pltpu.SemaphoreType.DMA((7,)),
            pltpu.SemaphoreType.DMA((len(held),)),
            pltpu.VMEM((512, 512), bf),
            pltpu.VMEM((SLABS, 32, 384), jnp.float32),
            pltpu.VMEM((H, 512, 256), bf),
            pltpu.VMEM((H + 2, 64, 512), bf),
            pltpu.VMEM((H + 1, 128, 512), bf),
            pltpu.VMEM((512, 48), bf),
            pltpu.VMEM((128, 512), bf),
            pltpu.VMEM((128, 896), bf),
            pltpu.VMEM((4, 128, 128), bf),
            pltpu.VMEM((256, 256), bf),
            pltpu.VMEM((32, 1024), bf),
            pltpu.VMEM((2, 4, 8 * H, 128), jnp.float32),
            pltpu.VMEM((128, 128), jnp.float32),
            pltpu.VMEM((128, 256), bf),
        ],
        compiler_params=pltpu.CompilerParams(vmem_limit_bytes=67043328 - (800 << 10)),
    )(*operands)
    return out.reshape(1, 1, 3, E * E * E)


def solution(mesh):
    flat = mesh.shape["blk"] == 8
    return jax.shard_map(
        flat_shards if flat else layered_shards,
        mesh=mesh,
        in_specs=(
            P("grp", "blk", None),
            P("grp", None, None),
            P("grp", None),
            P("grp", None),
            P("grp", "blk", None),
            P(),
            P(),
            P(),
            P(),
            P(),
            P(),
            P(),
            P(),
            P(),
            P(),
            P(),
            P(),
        ),
        out_specs=P("grp", "blk", None, None),
        check_vma=False,
    )
```

```python
import jax
import jax.numpy as jnp
import numpy as np
from jax import lax
from jax.experimental import pallas as pl
from jax.experimental.pallas import tpu as pltpu
from jax.sharding import PartitionSpec as P


E = 32


def from_behind(shard, axis, by):
    devices = lax.axis_size(axis)
    return lax.ppermute(shard, axis, [(i, (i + by) % devices) for i in range(devices)])


def extended(shard, sides, width):
    for axis, dim in sides:
        devices, length = (lax.axis_size(axis), shard.shape[dim])
        up = [(i, (i + 1) % devices) for i in range(devices - 1)]
        down = [(j, i) for i, j in up]
        last = lax.slice_in_dim(shard, length - width, length, axis=dim)
        initial = lax.slice_in_dim(shard, 0, width, axis=dim)
        before = lax.ppermute(last, axis, up)
        after = lax.ppermute(initial, axis, down)
        shard = jnp.concatenate([before, shard, after], axis=dim)
    return shard


def faces_of(x):
    return jnp.stack([x[:, 0], x[:, -1], x[:, :, 0], x[:, :, -1], x[:, :, :, 0], x[:, :, :, -1]])


def conv_taps(x, halos, weight):
    chans = x.shape[0]
    views = [
        x,
        jnp.concatenate([halos[0][:, None], x[:, :-1]], 1),
        jnp.concatenate([x[:, 1:], halos[1][:, None]], 1),
        jnp.concatenate([halos[2][:, :, None], x[:, :, :-1]], 2),
        jnp.concatenate([x[:, :, 1:], halos[3][:, :, None]], 2),
        jnp.concatenate([halos[4][:, :, :, None], x[:, :, :, :-1]], 3),
        jnp.concatenate([x[:, :, :, 1:], halos[5][:, :, :, None]], 3),
    ]
    total = jnp.dot(weight[0], views[0].reshape(chans, -1), preferred_element_type=jnp.float32)
    for tap in range(1, 7):
        total = total + jnp.dot(
            weight[tap], views[tap].reshape(chans, -1), preferred_element_type=jnp.float32
        )
    return total


def upsample(v, factor):
    chans, side = (v.shape[0], v.shape[1])
    big = jnp.broadcast_to(
        v[:, :, None, :, None, :, None], (chans, side, factor, side, factor, side, factor)
    )
    return big.reshape(chans, side * factor, side * factor, side * factor)


def pooled(a0):
    half = a0.shape[1] // 2
    return a0.reshape(a0.shape[0], half, 2, half, 2, half, 2).max(axis=(2, 4, 6))


def neighbour_faces(x, nbr):
    flat = faces_of(x)
    count = lax.axis_size("blk")
    depth_blocks = count // 8
    offsets = [-(count // 2), count // 2, -depth_blocks, depth_blocks, -1, 1]
    pieces = []
    for direction in range(6):
        pieces.append(from_behind(flat[direction ^ 1], "blk", -offsets[direction]))
    mask = (nbr >= 0).astype(jnp.bfloat16)
    return jnp.stack(pieces) * mask[:, None, None, None]


def context_term(near, bx, by, bz, w_ctx, coarse, depth_blocks):
    side = 4 * coarse
    chans = near.shape[-1]
    regions = near.reshape(3, side, side, depth_blocks * coarse, chans)
    middle = jnp.pad(regions[1], ((coarse, coarse), (coarse, coarse), (0, 0), (0, 0)))
    zoff = bz * coarse
    xoff = bx * coarse
    yoff = by * coarse
    zero = jnp.zeros((), jnp.int32)
    size = (coarse, coarse, coarse, chans)
    shift = jnp.int32(coarse)
    taps = [
        lax.dynamic_slice(middle, (xoff + shift, yoff + shift, zoff, zero), size),
        lax.dynamic_slice(middle, (xoff, yoff + shift, zoff, zero), size),
        lax.dynamic_slice(middle, (xoff + 2 * shift, yoff + shift, zoff, zero), size),
        lax.dynamic_slice(middle, (xoff + shift, yoff, zoff, zero), size),
        lax.dynamic_slice(middle, (xoff + shift, yoff + 2 * shift, zoff, zero), size),
        lax.dynamic_slice(regions[0], (xoff, yoff, zoff, zero), size),
        lax.dynamic_slice(regions[2], (xoff, yoff, zoff, zero), size),
    ]
    total = jnp.dot(taps[0].reshape(-1, chans), w_ctx[0], preferred_element_type=jnp.float32)
    for tap in range(1, 7):
        total = total + jnp.dot(
            taps[tap].reshape(-1, chans), w_ctx[tap], preferred_element_type=jnp.float32
        )
    return total.T.reshape(-1, coarse, coarse, coarse)


def layered_shards(
    image,
    context,
    tissue,
    owner,
    neighbours,
    w_in,
    b_in,
    w_down,
    b_down,
    w_ctx,
    w_mid,
    b_mid,
    w_skip,
    w_lift,
    b_up,
    w_out,
    b_out,
):
    half = E // 2
    coarse = E // 8
    depth_blocks = tissue.shape[1] // 8
    nbr = neighbours[0, 0]
    volume = image.reshape(1, E, E, E)
    pre = conv_taps(volume, neighbour_faces(volume, nbr), w_in) + b_in[:, None]
    a0 = jnp.maximum(pre, 0.0).astype(jnp.bfloat16).reshape(-1, E, E, E)
    p1 = pooled(a0)
    pre = conv_taps(p1, neighbour_faces(p1, nbr), w_down) + b_down[:, None]
    a1 = jnp.maximum(pre, 0.0).astype(jnp.bfloat16).reshape(-1, half, half, half)
    me = lax.axis_index("blk")
    pos = jnp.sum(jnp.where(owner[0] == me, tissue[0], 0))
    bx = pos // (4 * depth_blocks)
    by = pos // depth_blocks % 4
    bz = pos % depth_blocks
    near = extended(context, (("grp", 0),), 1)
    cterm = context_term(near, bx, by, bz, w_ctx, coarse, depth_blocks)
    pre = conv_taps(a1, neighbour_faces(a1, nbr), w_mid) + b_mid[:, None]
    pre = pre + upsample(cterm, 4).reshape(cterm.shape[0], -1)
    a2 = jnp.maximum(pre, 0.0).astype(jnp.bfloat16)
    lifted = jnp.dot(w_lift, a2, preferred_element_type=jnp.float32).reshape(-1, half, half, half)
    mixed = upsample(lifted, 2).reshape(lifted.shape[0], -1)
    mixed = (
        mixed
        + jnp.dot(w_skip, a0.reshape(a0.shape[0], -1), preferred_element_type=jnp.float32)
        + b_up[:, None]
    )
    hidden = jnp.maximum(mixed, 0.0).astype(jnp.bfloat16)
    logits = jnp.dot(w_out, hidden, preferred_element_type=jnp.float32) + b_out[:, None]
    return jax.nn.sigmoid(logits).reshape(1, 1, 3, E * E * E)


H = E // 2
REACH = 8
SLABS = H + 4
WIDE = E + 2 * REACH


def selections():
    row = np.arange(8 * SLABS)
    slab, kk = row // 8, row % 8
    offset = np.where(kk < 4, kk - 1, kk % 2)
    shift = np.where(kk < 4, 0, np.where(kk < 6, WIDE, 2 * WIDE))
    pick = 2 * (slab - 2) + offset + REACH + shift
    rows = pick[:, None] == np.arange(3 * WIDE)[None, :]
    return jnp.asarray(rows, jnp.bfloat16)


def tap_table(chans):
    table = -np.ones((32, 8), np.int32)
    for p in range(8):
        px, py, pz = p // 4, p // 2 % 2, p % 2
        same = (py * 2 + pz) * 8
        other_y, other_z = ((1 - py) * 2 + pz) * 8, (py * 2 + 1 - pz) * 8
        near, far_y, far_z = px + 1, 4 + px, 6 + px
        table[same + near, p] = 0
        table[same + px, p] = 1
        table[same + px + 2, p] = 2
        table[other_y + (far_y if py == 0 else near), p] = 3
        table[other_y + (near if py == 0 else far_y), p] = 4
        table[other_z + (far_z if pz == 0 else near), p] = 5
        table[other_z + (near if pz == 0 else far_z), p] = 6
    return jnp.asarray(np.repeat(table, chans, axis=1))


def three_terms(v):
    high = v.astype(jnp.bfloat16)
    rest = v - high.astype(jnp.float32)
    mid = rest.astype(jnp.bfloat16)
    low = (rest - mid.astype(jnp.float32)).astype(jnp.bfloat16)
    return [t.astype(jnp.float32) for t in (high, mid, low)]


def block_kernel(
    tissue_ref, owner_ref, nbr_ref, bo_ref,
    img_ref, other_ref, lo_ref, hi_ref, rows_ref, ctx_hbm, even_hbm, odd_hbm,
    win_hbm, b1_hbm, wdown_hbm, bd_hbm, wc_hbm, wmid_hbm, bm_hbm, skip_hbm, lift_hbm, bp_hbm, wout_hbm, tap_hbm,
    out_ref,
    win_ref, b1_ref, wdown_ref, bd_ref, wc_ref, wmid_ref, bm_ref, skip_ref, lift_ref, bp_ref, wout_ref, tap_ref,
    view_ref, view_sems, sems, split_ref, p_ref, a0_ref, p1_ref, a1_ref, k1_ref, kd_ref, wm_ref, ku_ref, wp_ref, wo_ref, l_ref, bup_ref, spread_ref,
):
    bf, f32 = jnp.bfloat16, jnp.float32
    copies = [
        pltpu.make_async_copy(src, dst, sems.at[i])
        for i, (src, dst) in enumerate(
            (
                (win_hbm, win_ref), (b1_hbm, b1_ref), (wdown_hbm, wdown_ref), (bd_hbm, bd_ref), (wc_hbm, wc_ref),
                (wmid_hbm, wmid_ref), (bm_hbm, bm_ref), (skip_hbm, skip_ref), (lift_hbm, lift_ref),
                (bp_hbm, bp_ref), (wout_hbm, wout_ref), (tap_hbm, tap_ref),
            )
        )
    ]
    for copy in copies:
        copy.start()
    me = lax.axis_index("blk")
    pos = jnp.int32(0)
    for j in range(tissue_ref.shape[1]):
        pos = pos + jnp.where(owner_ref[0, j] == me, tissue_ref[0, j], 0)
    bx, by = pos // 4, pos % 4
    oks = []
    for t, (dx, dy) in enumerate(((0, 0), (-1, 0), (1, 0), (0, -1), (0, 1), (0, 0), (0, 0))):
        x, y = bx + dx, by + dy
        oks.append((x >= 0) & (x < 4) & (y >= 0) & (y < 4) if dx or dy else None)
        x, y = jnp.clip(x, 0, 3), jnp.clip(y, 0, 3)
        source = ctx_hbm if t < 5 else (even_hbm, odd_hbm)[t - 5]
        copies.append(
            pltpu.make_async_copy(source.at[pl.ds(4 * x, 4), pl.ds(y, 1)], view_ref.at[t], view_sems.at[t])
        )
        copies[-1].start()
    first = nbr_ref[0, 0] >= 0
    second = nbr_ref[0, 1] >= 0
    left, right = nbr_ref[0, 2] >= 0, nbr_ref[0, 3] >= 0

    def iota(shape, dim):
        return lax.broadcasted_iota(jnp.int32, shape, dim)

    def dot(a, b):
        return jnp.dot(a, b, preferred_element_type=f32)

    cell = iota((512, 1), 0)
    y, z = cell >> 5, cell & (E - 1)
    to = ((y & 1) * 2 + (z & 1)) * 128 + (y >> 1) * H + (z >> 1)
    for part in range(4):
        at = slice(128 * part, 128 * part + 128)
        split_ref[at, :] = jnp.where(to[at] == iota((128, 512), 1), 1.0, 0.0).astype(bf)

    lo, hi = lo_ref[...].astype(f32), hi_ref[...].astype(f32)
    lo = jnp.where(left, lo, 0.0)
    hi = jnp.where(right, hi, 0.0)
    none = jnp.zeros_like(lo)
    other = other_ref[...].astype(f32)
    mid = jnp.concatenate([other[:REACH], img_ref[...].astype(f32), other[REACH:]], axis=0)
    field = jnp.concatenate([none, lo, mid, hi, none], axis=1)
    x = iota(field.shape, 0)
    field = jnp.where((x >= jnp.where(first, 0, REACH)) & (x < jnp.where(second, WIDE, WIDE - REACH)), field, 0.0)
    field = field.astype(bf)
    parts = [dot(field[:, 512 * j : 512 * j + 512], split_ref[...]) for j in range(4)]
    hz = iota((WIDE, 512), 1) & (H - 1)
    inside = iota((8 * SLABS, 128), 1) < 64
    for q in range(4):
        py, pz = q // 2, q % 2
        v = jnp.concatenate([part[:, 128 * q : 128 * q + 128] for part in parts], axis=1)
        ys = pltpu.roll(v, H if py == 1 else 512 - H, axis=1)
        zs = pltpu.roll(v, 1 if pz == 1 else 511, axis=1)
        zs = jnp.where(hz == (0 if pz == 1 else H - 1), 0.0, zs)
        v = dot(rows_ref[...], jnp.concatenate([v.astype(bf), ys.astype(bf), zs.astype(bf)], axis=0))
        p_ref[:, 8 * q : 8 * q + 8, 0:256] = v[:, 128:384].reshape(SLABS, 8, 256)
        edge = jnp.where(inside, v[:, 384:512], v[:, 0:128])
        p_ref[:, 8 * q : 8 * q + 8, 256:384] = edge.reshape(SLABS, 8, 128)

    for copy in copies:
        copy.wait()
    taps = jnp.concatenate([win_ref[...].astype(f32)] * 8, axis=1)
    tap = tap_ref[...]
    w1 = jnp.zeros(tap.shape, f32)
    for t in range(7):
        w1 = jnp.where(tap == t, taps[t : t + 1], w1)
    b1 = jnp.concatenate([b1_ref[...]] * 8, axis=1)
    k1_ref[...] = jnp.concatenate([w1] + three_terms(b1) + [jnp.zeros((13, 512), f32)], axis=0).T.astype(bf)
    for j, pair in enumerate(((1, 2), (3, 4), (5, 6), (0, None))):
        upper = wdown_ref[pair[0]].astype(f32)
        if pair[1] is None:
            lower = jnp.concatenate(three_terms(bd_ref[...]) + [jnp.zeros((61, 128), f32)], axis=0)
        else:
            lower = wdown_ref[pair[1]].astype(f32)
        kd_ref[:, 128 * j : 128 * j + 128] = jnp.concatenate([upper, lower], axis=0).T.astype(bf)
    for t in range(7):
        wm_ref[:, 128 * t : 128 * t + 128] = wmid_ref[(t + 1) % 7]
    skip = skip_ref[...].astype(f32).T
    skip = jnp.concatenate([skip, jnp.zeros_like(skip)], axis=1)
    wp_ref[0:128, 0:128] = skip.astype(bf)
    wp_ref[128:256, 0:128] = pltpu.roll(skip, 64, axis=1).astype(bf)
    wp_ref[0:128, 128:256] = lift_ref[...]
    wp_ref[128:256, 128:256] = lift_ref[...]
    bup_ref[...] = jnp.broadcast_to(bp_ref[...], (128, 128)).T
    head = jnp.concatenate([wout_ref[...].astype(f32), jnp.zeros((1, 128), f32)], axis=0)
    head = jnp.concatenate([head] * 8, axis=0)
    group = iota((32, 128), 0) >> 2
    for m in range(4):
        px, py = m // 2, m % 2
        wo_ref[:, 256 * m : 256 * m + 256] = jnp.concatenate(
            [jnp.where(group == (py * 2 + pz) * 2 + px, head, 0.0) for pz in range(2)], axis=1
        ).astype(bf)
    chan = iota((32, 256), 0) & 3
    b_out = jnp.where(chan == 0, bo_ref[0], jnp.where(chan == 1, bo_ref[1], bo_ref[2]))

    views = []
    for t in range(7):
        v = view_ref[t].reshape(64, 128)
        views.append(v if oks[t] is None else jnp.where(oks[t], v, jnp.zeros_like(v)))
    total = dot(views[0], wc_ref[0])
    for t in range(1, 5):
        total = total + dot(views[t], wc_ref[t])
    odd = lax.axis_index("grp") % 2
    total = total + dot(views[5], wc_ref[6 - odd]) + dot(views[6], wc_ref[5 + odd])
    terms = three_terms(total)
    bias = three_terms(bm_ref[...])
    for q in range(4):
        ku_ref[q] = jnp.concatenate(
            [t[16 * q : 16 * q + 16] for t in terms] + bias + [jnp.zeros((77, 128), f32)], axis=0
        ).T.astype(bf)

    ones = jnp.where(iota((16, 384), 0) < 3, 1.0, 0.0)
    near_x, next_x = jnp.where(first, 1, H + 2), jnp.where(first, 0, H + 3)
    zero = jnp.zeros((), bf)

    def keep(ok, v):
        return jnp.where(ok, v, jnp.zeros_like(v))

    lane = iota((48, 128), 1)
    outer = (lane < 32) | (lane >= 96)

    def full_res(i):
        slabs = tuple(range(4 * i, min(4 * i + 4, H + 2)))
        at = (near_x, next_x) if 4 * i == H else tuple(s + 2 for s in slabs)
        taps = [jnp.concatenate([p_ref[s], ones], axis=0) for s in at]
        edges = [
            jnp.where(outer, taps[k][:, 256:384], pltpu.roll(taps[k + 1][:, 256:384], 64, axis=1))
            for k in range(0, len(slabs), 2)
        ]
        taps = jnp.concatenate([t[:, 0:256] for t in taps] + edges, axis=1).astype(bf)
        a0 = jnp.maximum(dot(k1_ref[...], taps).astype(bf), zero)
        pool = a0[0:64]
        for p in range(1, 8):
            pool = jnp.maximum(pool, a0[64 * p : 64 * p + 64])
        for k, s in enumerate(slabs):
            if s < H:
                a0_ref[s] = a0[:, 256 * k : 256 * k + 256]
            base = 256 * len(slabs) + 128 * (k // 2)
            edge = pool[:, base : base + 128]
            if k % 2:
                edge = pltpu.roll(edge, 64, axis=1)
            p1_ref[s, :, 0:128] = keep(left, edge)
            p1_ref[s, :, 128:384] = pool[:, 256 * k : 256 * k + 256]
            p1_ref[s, :, 384:512] = keep(right, edge)

    def beside(ref, s, lanes):
        if 0 < s < H - 1:
            return ref[s - 1, :, lanes], ref[s + 1, :, lanes]
        if s == 0:
            return keep(first, ref[H, :, lanes]), ref[1, :, lanes]
        if s == H - 1:
            return ref[H - 2, :, lanes], keep(second, ref[H, :, lanes])
        behind, inside = ref[H + 1, :, lanes], jnp.where(first, ref[0, :, lanes], ref[H - 1, :, lanes])
        return jnp.where(first, behind, inside), jnp.where(first, inside, behind)

    hz = iota((64, 512), 1) & (H - 1)
    notfirst = jnp.where(hz == 0, 0.0, 1.0).astype(bf)
    notlast = jnp.where(hz == H - 1, 0.0, 1.0).astype(bf)
    extra = jnp.where(iota((64, 512), 0) < 3, 1.0, 0.0).astype(bf)

    inner = iota((512, 128), 1) < 64

    def half_res(i):
        slabs = tuple(range(2 * i, min(2 * i + 2, H + 1)))
        fields = []
        for s in slabs:
            mid = p1_ref[s]
            fields.append(
                jnp.concatenate(
                    [
                        *beside(p1_ref, s, slice(0, 512)), pltpu.roll(mid, H, axis=1), pltpu.roll(mid, 512 - H, axis=1),
                        pltpu.roll(mid, 1, axis=1) * notfirst, pltpu.roll(mid, 511, axis=1) * notlast, mid, extra,
                    ],
                    axis=0,
                )
            )
        edges = [jnp.where(inner, f[:, 384:512], f[:, 0:128]) for f in fields]
        a1 = jnp.maximum(dot(kd_ref[...], jnp.concatenate([f[:, 128:384] for f in fields] + edges, axis=1)).astype(bf), zero)
        for k, s in enumerate(slabs):
            edge = a1[:, 256 * len(slabs) + 128 * k : 256 * len(slabs) + 128 * k + 128]
            a1_ref[s, :, 0:128] = keep(left, edge)
            a1_ref[s, :, 128:384] = a1[:, 256 * k : 256 * k + 256]
            a1_ref[s, :, 384:512] = keep(right, edge)

    rows = iota((128, 256), 0)
    cols = iota((128, 256), 1)
    coarse = (cols >> 6) * 4 + ((cols & (H - 1)) >> 2)
    spread = jnp.where(rows < 48, jnp.where((rows & (H - 1)) == coarse, 1.0, 0.0), jnp.where(rows < 51, 1.0, 0.0))
    spread_ref[...] = spread.astype(bf)
    hz = cols & (H - 1)
    notfirst2 = jnp.where(hz == 0, 0.0, 1.0).astype(bf)
    notlast2 = jnp.where(hz == H - 1, 0.0, 1.0).astype(bf)

    def decode(h):
        wide = a1_ref[h]
        mid = wide[:, 128:384]
        field = jnp.concatenate(
            [
                *beside(a1_ref, h, slice(128, 384)),
                pltpu.roll(wide, H, axis=1)[:, 128:384], pltpu.roll(wide, 512 - H, axis=1)[:, 128:384],
                pltpu.roll(mid, 1, axis=1) * notfirst2, pltpu.roll(mid, 255, axis=1) * notlast2, mid, spread_ref[...],
            ],
            axis=0,
        )
        pre = dot(jnp.concatenate([wm_ref[...], ku_ref[h // 4]], axis=1), field)
        a2 = jnp.maximum(pre.astype(bf), zero)
        b_up = bup_ref[...]
        b_up = jnp.concatenate([b_up, b_up], axis=1)
        b_up = jnp.concatenate([b_up, b_up], axis=0)
        hidden = []
        for m in range(4):
            both = jnp.concatenate([a0_ref[h, 128 * m : 128 * m + 128, :], a2], axis=0)
            hidden.append(jnp.maximum((dot(wp_ref[...], both) + b_up).astype(bf), zero))
        logits = dot(wo_ref[...], jnp.concatenate(hidden, axis=0))
        logits = jax.nn.sigmoid(logits + b_out)
        for j in range(2):
            for q in range(4):
                l_ref[j, q, 8 * h : 8 * h + 8, :] = logits[
                    8 * q : 8 * q + 8, 128 * j : 128 * j + 128
                ]

    for stage, index in ORDER:
        (full_res, half_res, decode)[stage](index)

    v = jnp.concatenate(
        [
            jnp.concatenate([l_ref[j, q, pl.ds(c, E, stride=4), :] for q in range(4)], axis=1)
            for j in range(2)
            for c in range(3)
        ],
        axis=0,
    )
    high = v.astype(bf)
    rest = (v - high.astype(f32)).astype(bf)

    def back(t):
        return lax.dot_general(t, split_ref[...], (((1,), (1,)), ((), ())), preferred_element_type=f32)

    done = back(high) + back(rest)
    for j in range(2):
        for c in range(3):
            at = E * (3 * j + c)
            for b in range(4):
                out_ref[pl.ds(256 * c + 4 * j + b, E, stride=8), :] = done[at : at + E, 128 * b : 128 * b + 128]


ORDER = (
    [(0, H // 4)] + [(0, i) for i in range(H // 4)] + [(1, H // 2)] + [(1, i) for i in range(H // 2)] + [(2, h) for h in range(H)]
)


def flat_shards(
    image,
    context,
    tissue,
    owner,
    neighbours,
    w_in,
    b_in,
    w_down,
    b_down,
    w_ctx,
    w_mid,
    b_mid,
    w_skip,
    w_lift,
    b_up,
    w_out,
    b_out,
):
    bf = jnp.bfloat16
    count = lax.axis_size("blk")
    half = count // 2
    img = image.reshape(E, E * E)
    other = lax.ppermute(img, "blk", [(i, (i + half) % count) for i in range(count)])
    grp = lax.axis_size("grp")
    pairs = [[pair for i in range(odd, grp - 1, 2) for pair in ((i, i + 1), (i + 1, i))] for odd in range(2)]
    swap_a = lax.ppermute(context, "grp", pairs[1])
    swap_b = lax.ppermute(context, "grp", pairs[0])
    swaps = [swap_a, swap_b] if 1 == 0 else [swap_b, swap_a]

    def face(mid, side, lanes):
        return jnp.concatenate([side[E - REACH :, lanes], mid[:, lanes], side[:REACH, lanes]], axis=0)

    def turn(shard, by):
        return lax.ppermute(shard, "blk", [(i, i // half * half + (i + by) % half) for i in range(count)])

    high, low = slice((E - REACH) * E, E * E), slice(0, REACH * E)
    place = lax.axis_index("blk") % half
    lo = turn(jnp.where(place == half - 1, face(other, img, high), face(img, other, high)), 1)
    hi = turn(jnp.where(place == 0, face(other, img, low), face(img, other, low)), -1)

    rows = selections()
    grid4 = (16, 4, 16, context.shape[-1])
    vmem = pl.BlockSpec(memory_space=pltpu.VMEM)
    smem = pl.BlockSpec(memory_space=pltpu.SMEM)
    operands = (
        tissue, owner, neighbours[0], b_out,
        img, jnp.concatenate([other[E - REACH :], other[:REACH]], axis=0), lo, hi, rows,
        context.reshape(grid4), swaps[0].reshape(grid4), swaps[1].reshape(grid4),
        w_in[:, :, 0], b_in[None, :], jnp.swapaxes(w_down, 1, 2), b_down[None, :],
        w_ctx, w_mid, b_mid[None, :], w_skip.T, w_lift, b_up[None, :], w_out, tap_table(w_in.shape[1]),
    )
    held = operands[12:]
    out = pl.pallas_call(
        block_kernel,
        out_shape=jax.ShapeDtypeStruct((3 * E * E * E // 128, 128), jnp.float32),
        in_specs=[smem] * 4 + [vmem] * 5 + [pl.BlockSpec(memory_space=pltpu.HBM)] * (3 + len(held)),
        out_specs=vmem,
        scratch_shapes=[pltpu.VMEM(v.shape, v.dtype) for v in held]
        + [
            pltpu.VMEM((7, 4, 1, 16, context.shape[-1]), bf),
            pltpu.SemaphoreType.DMA((7,)),
            pltpu.SemaphoreType.DMA((len(held),)),
            pltpu.VMEM((512, 512), bf),
            pltpu.VMEM((SLABS, 32, 384), jnp.float32),
            pltpu.VMEM((H, 512, 256), bf),
            pltpu.VMEM((H + 2, 64, 512), bf),
            pltpu.VMEM((H + 1, 128, 512), bf),
            pltpu.VMEM((512, 48), bf),
            pltpu.VMEM((128, 512), bf),
            pltpu.VMEM((128, 896), bf),
            pltpu.VMEM((4, 128, 128), bf),
            pltpu.VMEM((256, 256), bf),
            pltpu.VMEM((32, 1024), bf),
            pltpu.VMEM((2, 4, 8 * H, 128), jnp.float32),
            pltpu.VMEM((128, 128), jnp.float32),
            pltpu.VMEM((128, 256), bf),
        ],
        compiler_params=pltpu.CompilerParams(vmem_limit_bytes=67043328 - (800 << 10)),
    )(*operands)
    return out.reshape(1, 1, 3, E * E * E)


def solution(mesh):
    flat = mesh.shape["blk"] == 8
    return jax.shard_map(
        flat_shards if flat else layered_shards,
        mesh=mesh,
        in_specs=(
            P("grp", "blk", None),
            P("grp", None, None),
            P("grp", None),
            P("grp", None),
            P("grp", "blk", None),
            P(),
            P(),
            P(),
            P(),
            P(),
            P(),
            P(),
            P(),
            P(),
            P(),
            P(),
            P(),
        ),
        out_specs=P("grp", "blk", None, None),
        check_vma=False,
    )
```
